32 devices in a mesh: cores: 2 (over core), row: 4 (over y, x), vec: 4 (over z).
Axes of the slice: x: 2, y: 2, z: 4, core: 2. Of those that a mesh axis runs over, the one named last changes fastest.
Arguments:
- train_cores: float32 [4, 512, 256, 256], P('vec', 'cores', 'row'), may hold values from -0.01953125 to 0.01953125
- sketch: float32 [512, 128], P('cores'), may hold values from -6 to 6
- exit_sketch: float32 [256, 128], replicated, may hold values from -6 to 6
Outputs:
- rounded: float32 [4, 256, 256, 128], P('vec', 'cores', 'row')
- interface_bases: float32 [4, 512, 128], P('vec', 'cores')
- margins: float32 [4, 256, 512], P('vec', 'cores')
The draws below stay inside these ranges and needn't reach their ends.
All inputs are finite; a program needn't handle non-finite values.
Results may differ from the reference program's by a relative error of at most 0.0003.
Values sent between devices are 32-bit elements; how exact they have to be, the bound alone decides.
No kernel may reach another device: no remote copies, remote signals or barrier semaphores. Data moves between devices by JAX's collectives and lax.ppermute only.
A program may use at most 192 MiB of HBM per device.

```python
import math
import jax
import jax.numpy as jnp
from jax import lax

MODE = 256
RANK = 256
TRUNC = 128
NCORE = 2
VECS = 4


def draw_train_cores(key, part):
    block_shape = (NCORE * RANK, MODE, RANK)
    common = jax.random.normal(jax.random.fold_in(key, 21), (1,) + block_shape, jnp.float32)
    separate = jax.random.normal(jax.random.fold_in(key, 22), (VECS,) + block_shape, jnp.float32)
    common_share = 0.85
    values = math.sqrt(common_share) * common + math.sqrt(1.0 - common_share) * separate
    return (jnp.clip(values, -5.0, 5.0) / math.sqrt(RANK * MODE)).astype(jnp.float32)


def level_of(key, dims, split, smallest, high):
    loudness = 1.0
    for axis_at, parts in split:
        heights = jax.random.uniform(jax.random.fold_in(jax.random.fold_in(key, 6), axis_at), (parts,), jnp.float32, smallest / len(split), high / len(split))
        loudness = loudness * jnp.repeat(jnp.exp(heights), dims[axis_at] // parts).reshape((-1,) + (1,) * (len(dims) - 1 - axis_at))
    return loudness


def noise(stream_key, shape, spread, reach, cuts=(), kind=jnp.bfloat16):
    entries = jax.random.normal(stream_key, shape, jnp.float32) * spread
    if len(cuts) > 0:
        entries = level_of(stream_key, shape, cuts, -0.22, 0.18) * entries
    return jnp.clip(entries, min=-reach, max=reach).astype(kind)


def setup_inputs(seed: int = 0) -> dict:
    seeds = jax.random.split(jax.random.key(seed), 4)
    train_cores = draw_train_cores(jax.random.fold_in(seeds[3], 71), 0)
    sketch = noise(seeds[1], (NCORE * RANK, TRUNC), 1.0, 6.0, ((0, 2),), jnp.float32)
    exit_sketch = noise(seeds[2], (RANK, TRUNC), 1.0, 6.0, (), jnp.float32)
    return {"train_cores": train_cores, "sketch": sketch, "exit_sketch": exit_sketch}


def product(left_mat, right_mat):
    return jnp.dot(left_mat.astype(jnp.float32), right_mat.astype(jnp.float32), precision=lax.Precision.HIGHEST, preferred_element_type=jnp.float32)

def orthonormal(gram_matrix, sketch):
    powered = product(gram_matrix, product(gram_matrix, sketch))
    chol_low = jnp.linalg.cholesky(product(powered.T, powered))
    return jax.scipy.linalg.solve_triangular(chol_low, powered.T, lower=True).T

def env_step(env_in, mine, others):
    carried = jnp.einsum('qzw,qwx->qzx', env_in, others, precision=lax.Precision.HIGHEST)
    carried = carried.reshape(others.shape[0], TRUNC * MODE, TRUNC)
    return jnp.einsum('cb,qcy->qby', mine.reshape(TRUNC * MODE, TRUNC), carried, precision=lax.Precision.HIGHEST)

def reference(train_cores, sketch, exit_sketch):
    identity = jnp.eye(RANK, dtype=jnp.float32)
    pieces_all = []
    frames_all = []
    for vector in range(VECS):
        lowers = []
        grams = []
        lower_prev = identity
        for position in range(NCORE):
            block_core = train_cores[vector, position * RANK:(position + 1) * RANK].reshape(RANK, MODE * RANK)
            absorbed = product(lower_prev.T, block_core).reshape(RANK * MODE, RANK)
            gram_matrix = product(absorbed.T, absorbed)
            lower_prev = jnp.linalg.cholesky(gram_matrix)
            lowers.append(lower_prev)
            grams.append(gram_matrix)
        incoming = orthonormal(grams[-1], exit_sketch)
        pieces = [None] * NCORE
        frames = [None] * NCORE
        for position in range(NCORE - 1, -1, -1):
            block_core = train_cores[vector, position * RANK:(position + 1) * RANK].reshape(RANK * MODE, RANK)
            if position == NCORE - 1:
                right_map = incoming
            else:
                right_map = jax.scipy.linalg.solve_triangular(lowers[position], incoming, lower=True, trans=1)
            outer = identity if position == 0 else lowers[position - 1]
            mixed_core = product(outer.T, product(block_core, right_map).reshape(RANK, MODE * TRUNC))
            frame = orthonormal(product(mixed_core, mixed_core.T), sketch[position * RANK:(position + 1) * RANK])
            pieces[position] = product(frame.T, mixed_core)
            frames[position] = frame
            incoming = frame
        pieces_all.append(pieces)
        frames_all.append(frames)
    margins = []
    firsts = jnp.stack([frames_all[other][0] for other in range(VECS)])
    for vector in range(VECS):
        env_in = jnp.einsum('az,qay->qzy', frames_all[vector][0], firsts, precision=lax.Precision.HIGHEST)
        blocks = []
        for position in range(NCORE):
            others = jnp.stack([pieces_all[other][position] for other in range(VECS)])
            env_in = env_step(env_in, pieces_all[vector][position], others)
            blocks.append(env_in.transpose(1, 0, 2).reshape(TRUNC, VECS * TRUNC))
        margins.append(jnp.concatenate(blocks, axis=0))
    rounded = jnp.stack([jnp.concatenate([piece.reshape(TRUNC, MODE, TRUNC) for piece in pieces_all[vector]], axis=0) for vector in range(VECS)])
    bases_out = jnp.stack([jnp.concatenate(frames_all[vector], axis=0) for vector in range(VECS)])
    return (rounded * math.sqrt(TRUNC * MODE), bases_out * math.sqrt(RANK), jnp.stack(margins))
```

```python
import functools
import math

import jax
import jax.numpy as jnp
from jax import lax
from jax.experimental import pallas as pl
from jax.experimental.pallas import tpu as pltpu
from jax.sharding import PartitionSpec as P

MODE = 256
F32 = jnp.float32
BF16 = jnp.bfloat16


def contract(left, right, left_dim, right_dim, precision=None):
    return lax.dot_general(
        left,
        right,
        (((left_dim,), (right_dim,)), ((), ())),
        precision=precision,
        preferred_element_type=F32,
    )


exact = functools.partial(contract, precision=lax.Precision.HIGHEST)


def split(value):
    high = value.astype(BF16)
    return high, (value - high.astype(F32)).astype(BF16)


def tree_sum(terms):
    terms = list(terms)
    while len(terms) > 1:
        terms = [terms[i] + terms[i + 1] for i in range(0, len(terms), 2)]
    return terms[0]


def shape(dims, dtype=F32):
    return jax.ShapeDtypeStruct(dims, dtype)


def fixed(*dims):
    return pl.BlockSpec(dims, lambda *_: (0,) * len(dims))


def inverse_factor(gram):
    size = gram.shape[0]
    row_id = lax.broadcasted_iota(jnp.int32, (size, size), 0)
    col_id = lax.broadcasted_iota(jnp.int32, (size, size), 1)
    inverse = jnp.where(row_id == col_id, 1.0, 0.0).astype(F32)
    finished = []
    for start in range(0, size, 8):
        left = size - start
        rows = row_id[:left]
        columns = [
            jnp.broadcast_to(gram[:, start + t : start + t + 1], (left, size)) for t in range(8)
        ]
        scale = jnp.zeros((8, size), F32)
        for t in range(8):
            pivot = columns[t][t : t + 1, :]
            factor = jnp.where(rows > t, columns[t] * (1.0 / pivot), 0.0)
            for s in range(t + 1, 8):
                columns[s] = columns[s] - factor * columns[s][t : t + 1, :]
            gram = gram - factor * gram[t : t + 1, :]
            inverse = inverse - factor * inverse[t : t + 1, :]
            scale = jnp.where(rows[:8] == t, lax.rsqrt(pivot), scale)
        finished.append(inverse[:8] * scale)
        gram = gram[8:]
        inverse = inverse[8:]
    return jnp.concatenate(finished, axis=0)


def gram_body(on_ref, core_ref, out_ref, acc_ref):
    step = pl.program_id(0)

    @pl.when(on_ref[0] == 1)
    def _():
        @pl.when(step == 0)
        def _():
            acc_ref[...] = jnp.zeros_like(acc_ref)

        rank, modes, width = core_ref.shape
        high, low = split(core_ref[...].reshape(rank * modes, width))
        acc_ref[...] += contract(high, jnp.concatenate([high, low], axis=1), 0, 0)

        @pl.when(step == pl.num_programs(0) - 1)
        def _():
            cross = acc_ref[:, width:]
            out_ref[...] = acc_ref[:, :width] + (cross + cross.T)


def core_spec(rank, modes, width):
    return pl.BlockSpec((rank, modes, width), lambda s, on: (0, s * on[0], 0))


def gram(on, core):
    rank, mode_count, width = core.shape
    modes = min(16, mode_count)
    return pl.pallas_call(
        gram_body,
        grid_spec=pltpu.PrefetchScalarGridSpec(
            num_scalar_prefetch=1,
            grid=(mode_count // modes,),
            in_specs=[core_spec(rank, modes, width)],
            out_specs=fixed(width, width),
            scratch_shapes=[pltpu.VMEM((width, 2 * width), F32)],
        ),
        out_shape=shape((width, width)),
        name="gram",
    )(on, core)


def absorbed_body(on_ref, outer_ref, core_ref, out_ref, both_ref, acc_ref, mid_ref):
    step = pl.program_id(0)

    @pl.when(on_ref[0] == 1)
    def _():
        rank, modes, width = core_ref.shape

        @pl.when(step == 0)
        def _():
            acc_ref[...] = jnp.zeros_like(acc_ref)
            outer_high, outer_low = split(outer_ref[...])
            both_ref[:rank] = outer_high
            both_ref[rank:] = outer_low

        high, low = split(core_ref[...].transpose(1, 0, 2))
        both = both_ref[...]
        for i in range(modes):
            stacked = contract(both, high[i], 1, 0)
            rest = contract(both[:rank], low[i], 1, 0)
            main = stacked[:rank] + stacked[rank:]
            main_high = main.astype(BF16)
            mid_ref[i * rank : (i + 1) * rank, :width] = main_high
            mid_ref[i * rank : (i + 1) * rank, width:] = (
                (main - main_high.astype(F32)) * 0.5 + rest
            ).astype(BF16)
        acc_ref[...] += contract(high.reshape(modes * rank, width), mid_ref[...], 0, 0)

        @pl.when(step == pl.num_programs(0) - 1)
        def _():
            half = acc_ref[:, :width] * 0.5 + acc_ref[:, width:]
            out_ref[...] = half + half.T


def absorbed_gram(on, outer, core):
    rank, mode_count, width = core.shape
    modes = min(8, mode_count)
    return pl.pallas_call(
        absorbed_body,
        grid_spec=pltpu.PrefetchScalarGridSpec(
            num_scalar_prefetch=1,
            grid=(mode_count // modes,),
            in_specs=[fixed(rank, rank), core_spec(rank, modes, width)],
            out_specs=fixed(width, width),
            scratch_shapes=[
                pltpu.VMEM((2 * rank, rank), BF16),
                pltpu.VMEM((width, 2 * width), F32),
                pltpu.VMEM((modes * rank, 2 * width), BF16),
            ],
        ),
        out_shape=shape((width, width)),
        name="absorbed_gram",
    )(on, outer, core)


def project_body(on_ref, core_ref, map_ref, high_ref, low_ref, out_ref, both_ref, acc_ref):
    step = pl.program_id(0)

    @pl.when(on_ref[0] == 1)
    def _():
        rank, modes, width = core_ref.shape
        kept = map_ref.shape[1]

        @pl.when(step == 0)
        def _():
            acc_ref[...] = jnp.zeros_like(acc_ref)
            map_high, map_low = split(map_ref[...])
            both_ref[:, :kept] = map_high
            both_ref[:, kept:] = map_low

        high, low = split(core_ref[...].reshape(rank * modes, width))
        both = both_ref[...]
        first = contract(high, both, 1, 0)
        second = contract(low, both, 1, 0)
        mixed = first[:, :kept] + (first[:, kept:] + second[:, :kept])
        mixed = mixed.reshape(rank, modes, kept).transpose(1, 0, 2)
        mixed = jnp.concatenate([mixed[i] for i in range(modes)], axis=1)
        mixed_high, mixed_low = split(mixed)
        high_ref[...] = mixed_high
        low_ref[...] = mixed_low
        acc_ref[...] += contract(
            mixed_high, jnp.concatenate([mixed_high, mixed_low], axis=0), 1, 1
        )

        @pl.when(step == pl.num_programs(0) - 1)
        def _():
            cross = acc_ref[:, rank:]
            out_ref[...] = acc_ref[:, :rank] + (cross + cross.T)


def project(on, core, right_map):
    rank, mode_count, width = core.shape
    kept = right_map.shape[1]
    modes = min(16, mode_count)
    wide = pl.BlockSpec((rank, modes * kept), lambda s, on: (0, s * on[0]))
    return pl.pallas_call(
        project_body,
        grid_spec=pltpu.PrefetchScalarGridSpec(
            num_scalar_prefetch=1,
            grid=(mode_count // modes,),
            in_specs=[core_spec(rank, modes, width), fixed(width, kept)],
            out_specs=[wide, wide, fixed(rank, rank)],
            scratch_shapes=[
                pltpu.VMEM((width, 2 * kept), BF16),
                pltpu.VMEM((rank, 2 * rank), F32),
            ],
        ),
        out_shape=[
            shape((rank, mode_count * kept), BF16),
            shape((rank, mode_count * kept), BF16),
            shape((rank, rank)),
        ],
        name="project",
    )(on, core, right_map)


def factor_body(on_ref, gram_ref, low_ref, inv_ref):
    @pl.when(on_ref[0] == 1)
    def _():
        half = gram_ref.shape[0] // 2
        first = gram_ref[:half, :half]
        cross = gram_ref[half:, :half]
        inv_first = inverse_factor(first)
        low_cross = exact(cross, inv_first, 1, 1)
        second = gram_ref[half:, half:] - exact(low_cross, low_cross, 1, 1)
        inv_second = inverse_factor(second)
        zero = jnp.zeros((half, half), F32)
        low_ref[:half, :half] = exact(first, inv_first, 1, 1)
        low_ref[:half, half:] = zero
        low_ref[half:, :half] = low_cross
        low_ref[half:, half:] = exact(second, inv_second, 1, 1)
        inv_ref[:half, :half] = inv_first
        inv_ref[:half, half:] = zero
        inv_ref[half:, :half] = -exact(inv_second, exact(low_cross, inv_first, 1, 0), 1, 0)
        inv_ref[half:, half:] = inv_second


SMEM = pl.BlockSpec(memory_space=pltpu.SMEM)


def factor(on, gram_matrix):
    return pl.pallas_call(
        factor_body,
        in_specs=[SMEM, pl.BlockSpec(memory_space=pltpu.VMEM)],
        out_shape=[shape(gram_matrix.shape)] * 2,
        name="factor",
    )(on, gram_matrix)


def basis_body(count, absorbed, on_ref, *refs):
    part_refs, refs = refs[:count], refs[count:]
    if absorbed:
        sketch_ref, low_ref, inv_ref, basis_ref, front_ref, map_ref = refs
    else:
        sketch_ref, basis_ref = refs

    @pl.when(on_ref[0] == 1)
    def _():
        total = tree_sum([ref[...] for ref in part_refs])
        if absorbed:
            lower = low_ref[...]
            total = exact(exact(lower, total, 0, 0), lower, 1, 0)
        powered = exact(total, exact(total, sketch_ref[...], 1, 0), 1, 0)
        inverse = inverse_factor(exact(powered, powered, 0, 0))
        frame = exact(powered, inverse, 1, 1)
        basis_ref[...] = frame
        if absorbed:
            front_ref[...] = exact(lower, frame, 1, 0)
            map_ref[...] = exact(inv_ref[...], frame, 0, 0)


def basis(on, parts, sketch, lower=None, inverse=None):
    absorbed = lower is not None
    operands = (*parts, sketch) + ((lower, inverse) if absorbed else ())
    return pl.pallas_call(
        functools.partial(basis_body, len(parts), absorbed),
        in_specs=[SMEM] + [pl.BlockSpec(memory_space=pltpu.VMEM)] * len(operands),
        out_shape=[shape(sketch.shape)] * (3 if absorbed else 1),
        name="basis",
    )(on, *operands)


def round_body(scale, pieces, state_ref, high_ref, low_ref, front_ref, *refs):
    old_ref = None
    if len(refs) == pieces + 3:
        old_ref, refs = refs[0], refs[1:]
    rounded_ref, piece_refs, both_ref = refs[0], refs[1 : pieces + 1], refs[pieces + 1]
    step = pl.program_id(0)
    kept = front_ref.shape[1]

    @pl.when(state_ref[0] == 1)
    def _():
        @pl.when(step == 0)
        def _():
            front_high, front_low = split(front_ref[...].T)
            both_ref[:kept] = front_high
            both_ref[kept:] = front_low

        both = both_ref[...]
        first = contract(both, high_ref[...], 1, 0)
        second = contract(both[:kept], low_ref[...], 1, 0)
        shaped = first[:kept] + (first[kept:] + second)
        for d in range(pieces):

            @pl.when(step == d)
            def _(d=d):
                piece_refs[d][...] = shaped

        modes = shaped.shape[1] // kept
        stacked = jnp.stack([shaped[:, i * kept : (i + 1) * kept] for i in range(modes)], axis=0)
        rounded_ref[:, 0] = stacked.transpose(1, 0, 2) * scale

    if old_ref is not None:

        @pl.when(state_ref[0] == 0)
        def _():
            rounded_ref[...] = old_ref[...]


def round_core(state, high, low, front, pieces, scale, old=None):
    rank, wide = high.shape
    kept = front.shape[1]
    modes = wide // kept // pieces

    def place(s, state):
        return state[1] ^ (s * state[0])

    in_specs = [
        pl.BlockSpec((rank, modes * kept), lambda s, state: (0, place(s, state))),
        pl.BlockSpec((rank, modes * kept), lambda s, state: (0, place(s, state))),
        fixed(rank, kept),
    ]
    block = pl.BlockSpec((kept, 1, modes, kept), lambda s, state: (0, place(s, state), 0, 0))
    operands = [state, high, low, front]
    if old is not None:
        in_specs.append(block)
        operands.append(old)
    return pl.pallas_call(
        functools.partial(round_body, scale, pieces),
        grid_spec=pltpu.PrefetchScalarGridSpec(
            num_scalar_prefetch=1,
            grid=(pieces,),
            in_specs=in_specs,
            out_specs=[block] + [fixed(kept, modes * kept)] * pieces,
            scratch_shapes=[pltpu.VMEM((2 * kept, rank), BF16)],
        ),
        out_shape=[shape((kept, pieces, modes, kept))] + [shape((kept, modes * kept))] * pieces,
        input_output_aliases={} if old is None else {4: 0},
        name="round_core",
    )(*operands)


def pair_list(count):
    return [(p, q) for p in range(count) for q in range(p, count)]


def margin_body(count, first, state_ref, *refs):
    piece_refs, refs = refs[:count], refs[count:]
    if first:
        frame_refs, refs = refs[:count], refs[count:]
        out_ref, stage_ref, env_ref, frame_stage_ref = refs
    else:
        env_in_ref, out_ref, stage_ref, env_ref = refs
    step = pl.program_id(0)
    pairs = pair_list(count)
    index_of = {pair: i for i, pair in enumerate(pairs)}

    @pl.when(state_ref[0] == 1)
    def _():
        me = state_ref[1]
        kept = piece_refs[0].shape[0]

        @pl.when(step == 0)
        def _():
            out_ref[...] = jnp.zeros_like(out_ref)
            if first:
                for d in range(count):
                    frame_stage_ref[me ^ d] = frame_refs[d][...]
            for i, (p, q) in enumerate(pairs):
                if first:
                    env = exact(frame_stage_ref[p], frame_stage_ref[q], 0, 0)
                else:
                    env = env_in_ref[i * kept : (i + 1) * kept]
                env_high, env_low = split(env)
                env_ref[q, p * kept : (p + 1) * kept] = env_high
                env_ref[q, (count + p) * kept : (count + p + 1) * kept] = env_low

        for d in range(count):
            stage_ref[me ^ d] = piece_refs[d][...]
        modes = piece_refs[0].shape[1] // kept

        def tall(value):
            return jnp.concatenate(
                [value[:, i * kept : (i + 1) * kept] for i in range(modes)], axis=0
            )

        highs, lows, carried = [], [], {}
        for q in range(count):
            high, low = split(stage_ref[q])
            highs.append(tall(high))
            lows.append(tall(low))
            rows = (q + 1) * kept
            env_high = env_ref[q, :rows]
            env_low = env_ref[q, count * kept : count * kept + rows]
            stacked = contract(jnp.concatenate([env_high, env_low], axis=0), high, 1, 0)
            moved = stacked[:rows] + (stacked[rows:] + contract(env_high, low, 1, 0))
            for p in range(q + 1):
                carried[p, q] = split(tall(moved[p * kept : (p + 1) * kept]))
        for p in range(count):
            partners = range(p, count)
            main = contract(
                highs[p],
                jnp.concatenate([carried[p, q][part] for part in (0, 1) for q in partners], axis=1),
                0,
                0,
            )
            cross = contract(
                lows[p], jnp.concatenate([carried[p, q][0] for q in partners], axis=1), 0, 0
            )
            width = len(partners) * kept
            total = main[:, :width] + (main[:, width:] + cross)
            for j, q in enumerate(partners):
                i = index_of[p, q]
                out_ref[i * kept : (i + 1) * kept] += total[:, j * kept : (j + 1) * kept]


def margin_terms(state, pieces, frames=None, env=None):
    count = len(pieces)
    kept, wide = pieces[0].shape
    chunk = min(4 * kept, wide)
    first = frames is not None
    total = count * (count + 1) // 2 * kept
    piece_spec = pl.BlockSpec((kept, chunk), lambda s, state: (0, s * state[0]))
    extra = list(frames) if first else [env]
    scratch = [
        pltpu.VMEM((count, kept, chunk), F32),
        pltpu.VMEM((count, 2 * count * kept, kept), BF16),
    ]
    if first:
        scratch.append(pltpu.VMEM((count, *frames[0].shape), F32))
    return pl.pallas_call(
        functools.partial(margin_body, count, first),
        grid_spec=pltpu.PrefetchScalarGridSpec(
            num_scalar_prefetch=1,
            grid=(wide // chunk,),
            in_specs=[piece_spec] * count + [fixed(*x.shape) for x in extra],
            out_specs=fixed(total, kept),
            scratch_shapes=scratch,
        ),
        out_shape=shape((total, kept)),
        name="margin_terms",
    )(state, *pieces, *extra)


def pick_body(count, state_ref, first_ref, last_ref, out_ref):
    kept = out_ref.shape[0]
    me = state_ref[1]

    def write(env_ref):
        for q in range(count):
            low, high = jnp.minimum(me, q), jnp.maximum(me, q)
            index = low * count - low * (low - 1) // 2 + high - low
            block = env_ref[pl.ds(pl.multiple_of(index * kept, kept), kept), :]
            block = jnp.where(me > q, block.T, block)
            out_ref[:, q * kept : (q + 1) * kept] = block

    @pl.when(state_ref[2] == 0)
    def _():
        write(first_ref)

    @pl.when(state_ref[2] == 1)
    def _():
        write(last_ref)


def pick(state, env_first, env_last, count):
    kept = env_first.shape[1]
    return pl.pallas_call(
        functools.partial(pick_body, count),
        in_specs=[SMEM] + [pl.BlockSpec(memory_space=pltpu.VMEM)] * 2,
        out_shape=shape((kept, count * kept)),
        name="pick",
    )(state, env_first, env_last)


def send(block, axis, size, distance, source, target):
    pairs = [(source * size + i, target * size + (i ^ distance)) for i in range(size)]
    return lax.ppermute(block, ("cores", axis), pairs)


def hand_over(block, source, target):
    return lax.ppermute(block, "cores", [(source, target)])


def shuffle(blocks, place):
    count = blocks.shape[0]
    for bit in range(count.bit_length() - 1):
        step = 1 << bit
        halves = blocks.reshape(count // (2 * step), 2, step, *blocks.shape[1:])
        turned = jnp.flip(halves, axis=1).reshape(blocks.shape)
        blocks = jnp.where((place >> bit) & 1 == 1, turned, blocks)
    return blocks


def scatter_sum(block, axis, size, place, core):
    parts = shuffle(block.reshape(size, block.shape[0] // size, block.shape[1]), place)
    return tree_sum([parts[0]] + [send(parts[d], axis, size, d, core, core) for d in range(1, size)])


def collect(block, axis, size, place, core):
    parts = jnp.stack([block] + [send(block, axis, size, d, core, core) for d in range(1, size)])
    return shuffle(parts, place).reshape(size * block.shape[0], block.shape[1])


def local(train_cores, sketch, exit_sketch):
    core = train_cores[0]
    rank, mode_count, _ = core.shape
    kept = sketch.shape[1]
    row_size = lax.axis_size("row")
    vec_size = lax.axis_size("vec")
    side = lax.axis_index("cores")
    row = lax.axis_index("row")
    vec = lax.axis_index("vec")
    on_first = (side == 0).astype(jnp.int32)[None]
    on_last = (side == 1).astype(jnp.int32)[None]
    state_first = jnp.stack([on_first[0], vec, side])
    state_last = jnp.stack([on_last[0], vec, side])
    scale = math.sqrt(kept * MODE)

    def row_parts(block, core_at):
        return [block] + [
            send(block, "row", row_size, d, core_at, core_at) for d in range(1, row_size)
        ]

    gram_first = gram(on_first, core)
    gram_all = tree_sum([send(gram_first, "row", row_size, d, 0, 1) for d in range(row_size)])
    gram_last = absorbed_gram(on_last, gram_all, core)
    lower, inverse = factor(on_first, hand_over(gram_all, 1, 0))
    lower = hand_over(lower, 0, 1)
    inverse = hand_over(inverse, 0, 1)
    (exit_frame,) = basis(on_last, row_parts(gram_last, 1), exit_sketch)
    last_high, last_low, left_last = project(on_last, core, exit_frame)
    frame_last, front, map_first = basis(
        on_last, row_parts(left_last, 1), sketch, lower, inverse
    )
    map_first = hand_over(map_first, 1, 0)
    first_high, first_low, left_first = project(on_first, core, map_first)
    rounded, *own_last = round_core(state_last, last_high, last_low, front, vec_size, scale)
    pieces_last = [own_last[0]] + [
        send(own_last[d], "vec", vec_size, d, 1, 1) for d in range(1, vec_size)
    ]
    (frame_first,) = basis(on_first, row_parts(left_first, 0), sketch)
    frames = [frame_first] + [
        send(frame_first, "vec", vec_size, d, 0, 0) for d in range(1, vec_size)
    ]
    rounded, *own_first = round_core(
        state_first, first_high, first_low, frame_first, vec_size, scale, rounded
    )
    pieces_first = [own_first[0]] + [
        send(own_first[d], "vec", vec_size, d, 0, 0) for d in range(1, vec_size)
    ]

    def total(env, core_at):
        env = scatter_sum(env, "row", row_size, row, core_at)
        env = scatter_sum(env, "vec", vec_size, vec, core_at)
        env = collect(env, "vec", vec_size, vec, core_at)
        return collect(env, "row", row_size, row, core_at)

    env_first = total(margin_terms(state_first, pieces_first, frames=frames), 0)
    env_last = margin_terms(state_last, pieces_last, env=hand_over(env_first, 0, 1))
    env_last = total(env_last, 1)
    margins = pick(state_first, env_first, env_last, vec_size)
    bases = jnp.where(side == 0, frame_first, frame_last) * math.sqrt(rank)
    return rounded.reshape(1, kept, mode_count, kept), bases[None], margins[None]


def solution(mesh):
    return jax.shard_map(
        local,
        mesh=mesh,
        in_specs=(P("vec", "cores", "row", None), P("cores", None), P()),
        out_specs=(
            P("vec", "cores", "row", None),
            P("vec", "cores", None),
            P("vec", "cores", None),
        ),
        check_vma=False,
    )
```

```python
import functools
import math

import jax
import jax.numpy as jnp
from jax import lax
from jax.experimental import pallas as pl
from jax.experimental.pallas import tpu as pltpu
from jax.sharding import PartitionSpec as P


MODE = 256
F32 = jnp.float32
BF16 = jnp.bfloat16
BASIS_UNROLL = 2


def contract(left, right, left_dim, right_dim, precision=None):
    return lax.dot_general(
        left,
        right,
        (((left_dim,), (right_dim,)), ((), ())),
        precision=precision,
        preferred_element_type=F32,
    )


exact = functools.partial(contract, precision=lax.Precision.HIGHEST)


def split(value):
    high = value.astype(BF16)
    return high, (value - high.astype(F32)).astype(BF16)


def tree_sum(terms):
    terms = list(terms)
    while len(terms) > 1:
        terms = [terms[i] + terms[i + 1] for i in range(0, len(terms), 2)]
    return terms[0]


def shape(dims, dtype=F32):
    return jax.ShapeDtypeStruct(dims, dtype)


def fixed(*dims):
    return pl.BlockSpec(dims, lambda *_: (0,) * len(dims))


def inverse_factor(gram, out_ref, unroll=1):
    size = gram.shape[0]
    row_id = lax.broadcasted_iota(jnp.int32, (size, size), 0)
    col_id = lax.broadcasted_iota(jnp.int32, (size, size), 1)
    inverse = jnp.where(row_id == col_id, 1.0, 0.0).astype(F32)
    done = 0
    while done < size:
        left = size - done
        panels = left // 16 if left > 16 * unroll else left // 8
        rows = row_id[:left]

        def panel(k, carry, left=left, done=done, rows=rows):
            gram, inverse = carry
            open_rows = rows < left - 8 * k
            columns = [jnp.broadcast_to(gram[:, t : t + 1], (left, size)) for t in range(8)]
            scale = jnp.zeros((8, size), F32)
            for t in range(8):
                pivot = columns[t][t : t + 1, :]
                factor = jnp.where((rows > t) & open_rows, columns[t] * (1.0 / pivot), 0.0)
                for s in range(t + 1, 8):
                    columns[s] = columns[s] - factor * columns[s][t : t + 1, :]
                gram = gram - factor * gram[t : t + 1, :]
                inverse = inverse - factor * inverse[t : t + 1, :]
                scale = jnp.where(rows[:8] == t, lax.rsqrt(pivot), scale)
            out_ref[pl.ds(pl.multiple_of(done + 8 * k, 8), 8), :] = inverse[:8] * scale
            gram = pltpu.roll(jnp.concatenate([gram[8:], gram[:8]], axis=0), size - 8, 1)
            return gram, jnp.concatenate([inverse[8:], inverse[:8]], axis=0)

        carry = (gram[:left], inverse[:left])
        gram, inverse = lax.fori_loop(0, panels, panel, carry, unroll=min(unroll, panels))
        done += 8 * panels
        gram, inverse = gram[: size - done], inverse[: size - done]


def write_halves(state_ref, value, keep_ref, give_ref):
    half = value.shape[0] // 2
    cut = half // 2
    first = jnp.concatenate([value[:half, :half], value[half : half + cut, :half]], axis=0)
    second = jnp.concatenate([value[half + cut :, :half], value[half:, half:]], axis=0)
    mine = state_ref[2] == 0
    keep_ref[...] = jnp.where(mine, first, second)
    give_ref[...] = jnp.where(mine, second, first)


def read_halves(state_ref, own_ref, other_ref):
    own, other = own_ref[...], other_ref[...]
    mine = state_ref[2] == 0
    first = jnp.where(mine, own, other)
    second = jnp.where(mine, other, own)
    half = own.shape[1]
    cut = half // 2
    cross = jnp.concatenate([first[half:], second[:cut]], axis=0)
    return first[:half], cross, second[cut:]


def whole(blocks):
    first, cross, second = blocks
    return jnp.concatenate(
        [jnp.concatenate([first, cross.T], axis=1), jnp.concatenate([cross, second], axis=1)],
        axis=0,
    )


def half_dims(rank):
    return (3 * rank // 4, rank // 2)


def gram_body(state_ref, core_ref, keep_ref, give_ref, acc_ref):
    step = pl.program_id(0)

    @pl.when(state_ref[0] == 1)
    def _():
        @pl.when(step == 0)
        def _():
            acc_ref[...] = jnp.zeros_like(acc_ref)

        rank, modes, width = core_ref.shape
        high, low = split(core_ref[...].reshape(rank * modes, width))
        acc_ref[...] += contract(high, jnp.concatenate([high, low], axis=1), 0, 0)

        @pl.when(step == pl.num_programs(0) - 1)
        def _():
            cross = acc_ref[:, width:]
            total = acc_ref[:, :width] + (cross + cross.T)
            write_halves(state_ref, total, keep_ref, give_ref)


def core_spec(rank, modes, width):
    return pl.BlockSpec((rank, modes, width), lambda s, state: (0, s * state[0], 0))


def gram(state, core):
    rank, mode_count, width = core.shape
    modes = min(16, mode_count)
    return pl.pallas_call(
        gram_body,
        grid_spec=pltpu.PrefetchScalarGridSpec(
            num_scalar_prefetch=1,
            grid=(mode_count // modes,),
            in_specs=[core_spec(rank, modes, width)],
            out_specs=[fixed(*half_dims(width))] * 2,
            scratch_shapes=[pltpu.VMEM((width, 2 * width), F32)],
        ),
        out_shape=[shape(half_dims(width))] * 2,
        name="gram",
    )(state, core)


def write_factor(state_ref, own_ref, other_ref, low_ref, inv_ref, work_ref):
    half = low_ref.shape[0] // 2
    first, cross, second = read_halves(state_ref, own_ref, other_ref)
    inverse_factor(first, work_ref)
    inv_first = work_ref[...]
    low_cross = exact(cross, inv_first, 1, 1)
    second = second - exact(low_cross, low_cross, 1, 1)
    inverse_factor(second, work_ref)
    inv_second = work_ref[...]
    zero = jnp.zeros((half, half), F32)
    low_ref[:half, :half] = exact(first, inv_first, 1, 1)
    low_ref[:half, half:] = zero
    low_ref[half:, :half] = low_cross
    low_ref[half:, half:] = exact(second, inv_second, 1, 1)
    inv_ref[:half, :half] = inv_first
    inv_ref[:half, half:] = zero
    inv_ref[half:, :half] = -exact(inv_second, exact(low_cross, inv_first, 1, 0), 1, 0)
    inv_ref[half:, half:] = inv_second


def absorbed_body(
    state_ref,
    own_ref,
    other_ref,
    core_ref,
    keep_ref,
    give_ref,
    low_ref,
    inv_ref,
    both_ref,
    acc_ref,
    mid_ref,
    work_ref,
):
    step = pl.program_id(0)

    @pl.when((state_ref[0] == 0) & (step == 0))
    def _():
        write_factor(state_ref, own_ref, other_ref, low_ref, inv_ref, work_ref)

    @pl.when(state_ref[0] == 1)
    def _():
        rank, modes, width = core_ref.shape

        @pl.when(step == 0)
        def _():
            acc_ref[...] = jnp.zeros_like(acc_ref)
            outer_high, outer_low = split(whole(read_halves(state_ref, own_ref, other_ref)))
            both_ref[:rank] = outer_high
            both_ref[rank:] = outer_low

        high, low = split(core_ref[...].transpose(1, 0, 2))
        both = both_ref[...]
        for i in range(modes):
            stacked = contract(both, high[i], 1, 0)
            rest = contract(both[:rank], low[i], 1, 0)
            main = stacked[:rank] + stacked[rank:]
            main_high = main.astype(BF16)
            mid_ref[i * rank : (i + 1) * rank, :width] = main_high
            mid_ref[i * rank : (i + 1) * rank, width:] = (
                (main - main_high.astype(F32)) * 0.5 + rest
            ).astype(BF16)
        acc_ref[...] += contract(high.reshape(modes * rank, width), mid_ref[...], 0, 0)

        @pl.when(step == pl.num_programs(0) - 1)
        def _():
            half = acc_ref[:, :width] * 0.5 + acc_ref[:, width:]
            write_halves(state_ref, half + half.T, keep_ref, give_ref)


def absorbed_gram(state, outer, core):
    rank, mode_count, width = core.shape
    modes = min(8, mode_count)
    return pl.pallas_call(
        absorbed_body,
        grid_spec=pltpu.PrefetchScalarGridSpec(
            num_scalar_prefetch=1,
            grid=(mode_count // modes,),
            in_specs=[fixed(*half_dims(rank))] * 2 + [core_spec(rank, modes, width)],
            out_specs=[fixed(*half_dims(width))] * 2 + [fixed(rank, rank)] * 2,
            scratch_shapes=[
                pltpu.VMEM((2 * rank, rank), BF16),
                pltpu.VMEM((width, 2 * width), F32),
                pltpu.VMEM((modes * rank, 2 * width), BF16),
                pltpu.VMEM((rank // 2, rank // 2), F32),
            ],
        ),
        out_shape=[shape(half_dims(width))] * 2 + [shape((rank, rank))] * 2,
        name="absorbed_gram",
    )(state, *outer, core)


def project_step(state_ref, core_ref, map_ref, high_ref, low_ref, keep_ref, give_ref, both_ref, acc_ref):
    step = pl.program_id(0)
    rank, modes, width = core_ref.shape
    kept = map_ref.shape[1]

    @pl.when(step == 0)
    def _():
        acc_ref[...] = jnp.zeros_like(acc_ref)
        map_high, map_low = split(map_ref[...])
        both_ref[:, :kept] = map_high
        both_ref[:, kept:] = map_low

    high, low = split(core_ref[...].reshape(rank * modes, width))
    both = both_ref[...]
    first = contract(high, both, 1, 0)
    second = contract(low, both, 1, 0)
    mixed = first[:, :kept] + (first[:, kept:] + second[:, :kept])
    mixed = mixed.reshape(rank, modes, kept).transpose(1, 0, 2)
    mixed = jnp.concatenate([mixed[i] for i in range(modes)], axis=1)
    mixed_high, mixed_low = split(mixed)
    high_ref[...] = mixed_high
    low_ref[...] = mixed_low
    acc_ref[...] += contract(mixed_high, jnp.concatenate([mixed_high, mixed_low], axis=0), 1, 1)

    @pl.when(step == pl.num_programs(0) - 1)
    def _():
        cross = acc_ref[:, rank:]
        total = acc_ref[:, :rank] + (cross + cross.T)
        write_halves(state_ref, total, keep_ref, give_ref)


def shaped_piece(front_ref, high_ref, low_ref):
    kept = front_ref.shape[1]
    front_high, front_low = split(front_ref[...].T)
    both = jnp.concatenate([front_high, front_low], axis=0)
    first = contract(both, high_ref[...], 1, 0)
    second = contract(front_high, low_ref[...], 1, 0)
    return first[:kept] + (first[kept:] + second)


def project_body(pieces, state_ref, *refs):
    core_ref, map_ref, refs = refs[0], refs[1], refs[2:]
    if pieces:
        other_refs, refs = refs[:3], refs[3:]
        piece_refs, slots_ref, copied = refs[4 : 4 + pieces], refs[-2], refs[-1]
    high_ref, low_ref, keep_ref, give_ref = refs[:4]
    both_ref, acc_ref = refs[4 + pieces : 6 + pieces]

    @pl.when(state_ref[0] == 1)
    def _():
        project_step(
            state_ref, core_ref, map_ref, high_ref, low_ref, keep_ref, give_ref, both_ref, acc_ref
        )

    if pieces:

        @pl.when(state_ref[0] == 0)
        def _():
            step = pl.program_id(0)
            slots_ref[step] = shaped_piece(*other_refs)
            copies = [
                pltpu.make_async_copy(slots_ref.at[d], piece_refs[d], copied.at[d])
                for d in range(pieces)
            ]
            for d in range(pieces):

                @pl.when(step == d)
                def _(d=d):
                    copies[d].start()

            @pl.when(step == pieces - 1)
            def _():
                for copy in copies:
                    copy.wait()


def project(state, core, right_map, other=None, pieces=0):
    rank, mode_count, width = core.shape
    kept = right_map.shape[1]
    modes = mode_count // pieces if pieces else min(16, mode_count)
    wide = pl.BlockSpec((rank, modes * kept), lambda s, state: (0, s * state[0]))
    in_specs = [core_spec(rank, modes, width), fixed(width, kept)]
    out_specs = [wide, wide] + [fixed(*half_dims(rank))] * 2
    out_shape = [shape((rank, mode_count * kept), BF16)] * 2 + [shape(half_dims(rank))] * 2
    scratch = [pltpu.VMEM((width, 2 * kept), BF16), pltpu.VMEM((rank, 2 * rank), F32)]
    operands = [core, right_map]
    if pieces:
        away = pl.BlockSpec(
            (rank, modes * kept), lambda s, state: (0, state[1] ^ (s * (1 - state[0])))
        )
        in_specs += [fixed(rank, kept), away, away]
        operands += other
        out_specs += [pl.BlockSpec(memory_space=pl.ANY)] * pieces
        out_shape += [shape((kept, modes * kept))] * pieces
        scratch += [
            pltpu.VMEM((pieces, kept, modes * kept), F32),
            pltpu.SemaphoreType.DMA((pieces,)),
        ]
    return pl.pallas_call(
        functools.partial(project_body, pieces),
        grid_spec=pltpu.PrefetchScalarGridSpec(
            num_scalar_prefetch=1,
            grid=(mode_count // modes,),
            in_specs=in_specs,
            out_specs=out_specs,
            scratch_shapes=scratch,
        ),
        out_shape=out_shape,
        name="project",
    )(state, *operands)


SMEM = pl.BlockSpec(memory_space=pltpu.SMEM)
VMEM = pl.BlockSpec(memory_space=pltpu.VMEM)


def basis_body(absorbed, state_ref, own_ref, other_ref, *refs):
    if absorbed:
        sketch_ref, low_ref, inv_ref, basis_ref, front_ref, map_ref, work_ref = refs
    else:
        sketch_ref, basis_ref, work_ref = refs

    @pl.when(state_ref[0] == 1)
    def _():
        total = whole(read_halves(state_ref, own_ref, other_ref))
        if absorbed:
            lower = low_ref[...]
            total = exact(exact(lower, total, 0, 0), lower, 1, 0)
        powered = exact(total, exact(total, sketch_ref[...], 1, 0), 1, 0)
        inverse_factor(exact(powered, powered, 0, 0), work_ref, BASIS_UNROLL)
        frame = exact(powered, work_ref[...], 1, 1)
        basis_ref[...] = frame
        if absorbed:
            front_ref[...] = exact(lower, frame, 1, 0)
            map_ref[...] = exact(inv_ref[...], frame, 0, 0)


def basis(state, halves, sketch, lower=None, inverse=None):
    absorbed = lower is not None
    operands = (*halves, sketch) + ((lower, inverse) if absorbed else ())
    kept = sketch.shape[1]
    return pl.pallas_call(
        functools.partial(basis_body, absorbed),
        in_specs=[SMEM] + [VMEM] * len(operands),
        out_shape=[shape(sketch.shape)] * (3 if absorbed else 1),
        scratch_shapes=[pltpu.VMEM((kept, kept), F32)],
        name="basis",
    )(state, *operands)


def piece_body(state_ref, front_ref, high_ref, low_ref, piece_ref):
    @pl.when(state_ref[0] == 1)
    def _():
        piece_ref[...] = shaped_piece(front_ref, high_ref, low_ref)


def round_piece(state, front, high, low, pieces):
    rank, wide = high.shape
    kept = front.shape[1]
    width = wide // pieces
    parts = 2 if width % 2048 == 0 else 1
    block = pl.BlockSpec(
        (rank, width // parts), lambda s, state: (0, (state[1] * parts + s) * state[0])
    )
    return pl.pallas_call(
        piece_body,
        grid_spec=pltpu.PrefetchScalarGridSpec(
            num_scalar_prefetch=1,
            grid=(parts,),
            in_specs=[fixed(rank, kept), block, block],
            out_specs=pl.BlockSpec((kept, width // parts), lambda s, state: (0, s * state[0])),
        ),
        out_shape=shape((kept, width)),
        name="round_piece",
    )(state, front, high, low)


def layout_body(pieces, scale, state_ref, *refs):
    sides, (out_ref, slots_ref, laid_ref, taken, placed) = (
        (refs[:pieces], refs[pieces : 2 * pieces]),
        refs[2 * pieces :],
    )
    vec = state_ref[1]
    for side in (0, 1):

        @pl.when(state_ref[2] == side)
        def _(side=side):
            copies = [
                pltpu.make_async_copy(sides[side][d], slots_ref.at[d], taken.at[d])
                for d in range(pieces)
            ]
            for copy in copies:
                copy.start()
            for copy in copies:
                copy.wait()

    kept, modes = laid_ref.shape[1:3]
    copies = []
    for d in range(pieces):
        stacked = jnp.stack(
            [slots_ref[d, :, i * kept : (i + 1) * kept] for i in range(modes)], axis=0
        )
        laid_ref[d] = stacked.transpose(1, 0, 2) * scale
        copies.append(pltpu.make_async_copy(laid_ref.at[d], out_ref.at[:, vec ^ d], placed.at[d]))
        copies[-1].start()
    for copy in copies:
        copy.wait()


def lay_out(state, first, last, scale):
    pieces = len(first)
    kept, width = first[0].shape
    modes = width // kept
    anywhere = pl.BlockSpec(memory_space=pl.ANY)
    return pl.pallas_call(
        functools.partial(layout_body, pieces, scale),
        in_specs=[SMEM] + [anywhere] * (2 * pieces),
        out_specs=anywhere,
        out_shape=shape((kept, pieces, modes, kept)),
        scratch_shapes=[
            pltpu.VMEM((pieces, kept, width), F32),
            pltpu.VMEM((pieces, kept, modes, kept), F32),
            pltpu.SemaphoreType.DMA((pieces,)),
            pltpu.SemaphoreType.DMA((pieces,)),
        ],
        name="lay_out",
    )(state, *first, *last)


def pair_list(count):
    return [(p, q) for p in range(count) for q in range(p, count)]


def place_chunks(state_ref, own_ref, other_ref, out_ref):
    chunks, size = own_ref.shape[:2]
    side, row = state_ref[2], state_ref[3]
    for d in range(chunks):
        for ref, half in ((own_ref, side), (other_ref, 1 - side)):
            start = pl.multiple_of((half * chunks + (row ^ d)) * size, 8)
            out_ref[pl.ds(start, size), :] = ref[d]


def margin_body(count, first, state_ref, *refs):
    piece_refs, refs = refs[:count], refs[count:]
    if first:
        frame_refs, refs = refs[:count], refs[count:]
        keep_ref, give_ref, stage_ref, env_ref, out_ref, frame_stage_ref = refs
    else:
        own_ref, other_ref, keep_ref, give_ref, stage_ref, env_ref, out_ref, env_in_ref = refs
    step = pl.program_id(0)
    pairs = pair_list(count)
    index_of = {pair: i for i, pair in enumerate(pairs)}

    @pl.when(state_ref[0] == 1)
    def _():
        me = state_ref[1]
        kept = piece_refs[0].shape[0]

        @pl.when(step == 0)
        def _():
            out_ref[...] = jnp.zeros_like(out_ref)
            if first:
                for d in range(count):
                    frame_stage_ref[me ^ d] = frame_refs[d][...]
            else:
                place_chunks(state_ref, own_ref, other_ref, env_in_ref)
            for i, (p, q) in enumerate(pairs):
                if first:
                    env = exact(frame_stage_ref[p], frame_stage_ref[q], 0, 0)
                else:
                    env = env_in_ref[i * kept : (i + 1) * kept]
                env_high, env_low = split(env)
                env_ref[q, p * kept : (p + 1) * kept] = env_high
                env_ref[q, (count + p) * kept : (count + p + 1) * kept] = env_low

        for d in range(count):
            stage_ref[me ^ d] = piece_refs[d][...]
        modes = piece_refs[0].shape[1] // kept

        def tall(value):
            return jnp.concatenate(
                [value[:, i * kept : (i + 1) * kept] for i in range(modes)], axis=0
            )

        highs, lows, carried = [], [], {}
        for q in range(count):
            high, low = split(stage_ref[q])
            highs.append(tall(high))
            lows.append(tall(low))
            rows = (q + 1) * kept
            env_high = env_ref[q, :rows]
            env_low = env_ref[q, count * kept : count * kept + rows]
            stacked = contract(jnp.concatenate([env_high, env_low], axis=0), high, 1, 0)
            moved = stacked[:rows] + (stacked[rows:] + contract(env_high, low, 1, 0))
            for p in range(q + 1):
                carried[p, q] = split(tall(moved[p * kept : (p + 1) * kept]))
        for p in range(count):
            partners = range(p, count)
            main = contract(
                jnp.concatenate([highs[p], lows[p]], axis=1),
                jnp.concatenate([carried[p, q][0] for q in partners], axis=1),
                0,
                0,
            )
            cross = contract(
                highs[p], jnp.concatenate([carried[p, q][1] for q in partners], axis=1), 0, 0
            )
            total = main[:kept] + (main[kept:] + cross)
            for j, q in enumerate(partners):
                i = index_of[p, q]
                out_ref[i * kept : (i + 1) * kept] += total[:, j * kept : (j + 1) * kept]

        @pl.when(step == pl.num_programs(0) - 1)
        def _():
            chunks, size = keep_ref.shape[:2]
            side, row = state_ref[2], state_ref[3]
            for d in range(chunks):
                for ref, half in ((keep_ref, side), (give_ref, 1 - side)):
                    start = pl.multiple_of((half * chunks + (row ^ d)) * size, 8)
                    ref[d] = out_ref[pl.ds(start, size), :]


def margin_terms(state, pieces, rows, frames=None, env=None):
    count = len(pieces)
    kept, wide = pieces[0].shape
    chunk = min(4 * kept, wide)
    first = frames is not None
    total = count * (count + 1) // 2 * kept
    piece_spec = pl.BlockSpec((kept, chunk), lambda s, state: (0, s * state[0]))
    extra = list(frames) if first else list(env)
    part = (rows, total // (2 * rows), kept)
    scratch = [
        pltpu.VMEM((count, kept, chunk), F32),
        pltpu.VMEM((count, 2 * count * kept, kept), BF16),
        pltpu.VMEM((total, kept), F32),
        pltpu.VMEM((count, *frames[0].shape) if first else (total, kept), F32),
    ]
    return pl.pallas_call(
        functools.partial(margin_body, count, first),
        grid_spec=pltpu.PrefetchScalarGridSpec(
            num_scalar_prefetch=1,
            grid=(wide // chunk,),
            in_specs=[piece_spec] * count + [fixed(*x.shape) for x in extra],
            out_specs=[fixed(*part)] * 2,
            scratch_shapes=scratch,
        ),
        out_shape=[shape(part)] * 2,
        name="margin_terms",
    )(state, *pieces, *extra)


def pick_body(count, state_ref, *refs):
    out_ref, env_ref = refs[4:]
    kept = out_ref.shape[0]
    me = state_ref[1]
    for side in (0, 1):

        @pl.when(state_ref[2] == side)
        def _(side=side):
            place_chunks(state_ref, refs[2 * side], refs[2 * side + 1], env_ref)

    for q in range(count):
        low, high = jnp.minimum(me, q), jnp.maximum(me, q)
        index = low * count - low * (low - 1) // 2 + high - low
        block = env_ref[pl.ds(pl.multiple_of(index * kept, kept), kept), :]
        block = jnp.where(me > q, block.T, block)
        out_ref[:, q * kept : (q + 1) * kept] = block


def pick(state, env_first, env_last, count):
    kept = env_first[0].shape[2]
    return pl.pallas_call(
        functools.partial(pick_body, count),
        in_specs=[SMEM] + [VMEM] * 4,
        out_shape=shape((kept, count * kept)),
        scratch_shapes=[pltpu.VMEM((count * (count + 1) // 2 * kept, kept), F32)],
        name="pick",
    )(state, *env_first, *env_last)


def send(block, axis, size, distance):
    return lax.ppermute(block, axis, [(i, i ^ distance) for i in range(size)])


def swap(block):
    return send(block, "cores", 2, 1)


def send_from(block, side, size, distance):
    pairs = [(side * size + i, side * size + (i ^ distance)) for i in range(size)]
    return lax.ppermute(block, ("cores", "vec"), pairs)


def exchange_sum(block, axis, size):
    return tree_sum([block] + [send(block, axis, size, d) for d in range(1, size)])


def local(train_cores, sketch, exit_sketch):
    core = train_cores[0]
    rank, mode_count, _ = core.shape
    kept = sketch.shape[1]
    row_size = lax.axis_size("row")
    vec_size = lax.axis_size("vec")
    side = lax.axis_index("cores")
    row = lax.axis_index("row")
    vec = lax.axis_index("vec")
    first_side = (side == 0).astype(jnp.int32)
    state_first = jnp.stack([first_side, vec, side, row])
    state_last = jnp.stack([1 - first_side, vec, side, row])
    state_both = jnp.stack([jnp.int32(1), vec, side, row])
    scale = math.sqrt(kept * MODE)

    def row_total(keep, give, holder):
        mine = jnp.where(side == holder, keep, swap(give))
        own = exchange_sum(mine, "row", row_size)
        return own, swap(own)

    def env_total(keep, give, holder):
        mine = jnp.where(side == holder, keep, swap(give))
        parts = [mine[0]] + [send(mine[d], "row", row_size, d) for d in range(1, row_size)]
        chunk = exchange_sum(tree_sum(parts), "vec", vec_size)
        own = jnp.stack([chunk] + [send(chunk, "row", row_size, d) for d in range(1, row_size)])
        return own, swap(own)

    def at(state, d):
        return state.at[1].set(vec ^ d)

    def sent(pieces, holder):
        out = [pieces[0]]
        for d in range(1, vec_size):
            out.append(send_from(pieces[d], holder, vec_size, d))
        return out

    gram_first = row_total(*gram(state_first, core), 0)
    *gram_last, lower, inverse = absorbed_gram(state_last, gram_first, core)
    gram_last = row_total(*gram_last, 1)
    lower = jnp.where(side == 0, lower, swap(lower))
    inverse = jnp.where(side == 0, inverse, swap(inverse))
    (exit_frame,) = basis(state_last, gram_last, exit_sketch)
    last_high, last_low, *left_last = project(state_last, core, exit_frame)
    left_last = row_total(*left_last, 1)
    other_sketch = swap(sketch)
    frame_last, front, map_first = basis(
        state_both, left_last, jnp.where(side == 1, sketch, other_sketch), lower, inverse
    )
    rounded_last = [front, last_high, last_low]
    if mode_count // vec_size % 8 == 0:
        first_high, first_low, *rest = project(
            state_first, core, map_first, rounded_last, vec_size
        )
        left_first, own_last = rest[:2], rest[2:]
    else:
        first_high, first_low, *left_first = project(state_first, core, map_first)
        own_last = [
            round_piece(at(state_last, d), *rounded_last, vec_size) for d in range(vec_size)
        ]
    left_first = row_total(*left_first, 0)
    *own_last, left_own, left_other = lax.optimization_barrier((*own_last, *left_first))
    pieces_last = sent(own_last, 1)
    (frame_first,) = basis(state_first, (left_own, left_other), sketch)
    own_first = [None] * vec_size
    for d in range(vec_size - 1, -1, -1):
        own_first[d] = round_piece(at(state_first, d), frame_first, first_high, first_low, vec_size)
    pieces_first = sent(own_first, 0)
    rounded = lay_out(state_both, own_first, own_last, scale)
    frames = [frame_first] + [send_from(frame_first, 0, vec_size, d) for d in range(1, vec_size)]
    env_first = env_total(*margin_terms(state_first, pieces_first, row_size, frames=frames), 0)
    env_last = env_total(*margin_terms(state_last, pieces_last, row_size, env=env_first), 1)
    margins = pick(state_both, env_first, env_last, vec_size)
    bases = jnp.where(side == 0, frame_first, frame_last) * math.sqrt(rank)
    return rounded.reshape(1, kept, mode_count, kept), bases[None], margins[None]


def solution(mesh):
    return jax.shard_map(
        local,
        mesh=mesh,
        in_specs=(P("vec", "cores", "row", None), P("cores", None), P()),
        out_specs=(
            P("vec", "cores", "row", None),
            P("vec", "cores", None),
            P("vec", "cores", None),
        ),
        check_vma=False,
    )
```

```python
import functools
import math

import jax
import jax.numpy as jnp
from jax import lax
from jax.experimental import pallas as pl
from jax.experimental.pallas import tpu as pltpu
from jax.sharding import PartitionSpec as P


MODE = 256
F32 = jnp.float32
BF16 = jnp.bfloat16


def contract(left, right, left_dim, right_dim, precision=None):
    return lax.dot_general(
        left,
        right,
        (((left_dim,), (right_dim,)), ((), ())),
        precision=precision,
        preferred_element_type=F32,
    )


exact = functools.partial(contract, precision=lax.Precision.HIGHEST)


def split(value):
    high = value.astype(BF16)
    return high, (value - high.astype(F32)).astype(BF16)


def tree_sum(terms):
    terms = list(terms)
    while len(terms) > 1:
        terms = [terms[i] + terms[i + 1] for i in range(0, len(terms), 2)]
    return terms[0]


def shape(dims, dtype=F32):
    return jax.ShapeDtypeStruct(dims, dtype)


def fixed(*dims):
    return pl.BlockSpec(dims, lambda *_: (0,) * len(dims))


def inverse_factor(gram, out_ref, unrolled=False):
    size = gram.shape[0]
    row_id = lax.broadcasted_iota(jnp.int32, (size, size), 0)
    col_id = lax.broadcasted_iota(jnp.int32, (size, size), 1)
    inverse = jnp.where(row_id == col_id, 1.0, 0.0).astype(F32)

    def eliminate(gram, inverse, column, open_rows):
        left = gram.shape[0]
        rows = row_id[:left]
        columns = [
            jnp.broadcast_to(gram[:, column + t : column + t + 1], (left, size)) for t in range(8)
        ]
        scale = jnp.zeros((8, size), F32)
        for t in range(8):
            pivot = columns[t][t : t + 1, :]
            use = rows > t
            if open_rows is not None:
                use = use & open_rows
            factor = jnp.where(use, columns[t] * (1.0 / pivot), 0.0)
            for s in range(t + 1, 8):
                columns[s] = columns[s] - factor * columns[s][t : t + 1, :]
            gram = gram - factor * gram[t : t + 1, :]
            inverse = inverse - factor * inverse[t : t + 1, :]
            scale = jnp.where(rows[:8] == t, lax.rsqrt(pivot), scale)
        return gram, inverse, inverse[:8] * scale

    if unrolled:
        for start in range(0, size, 8):
            gram, inverse, rows = eliminate(gram, inverse, start, None)
            out_ref[start : start + 8, :] = rows
            gram, inverse = gram[8:], inverse[8:]
        return

    done = 0
    while done < size:
        left = size - done
        panels = left // 16 if left > 16 else left // 8

        def panel(k, carry, left=left, done=done):
            gram, inverse = carry
            gram, inverse, rows = eliminate(gram, inverse, 0, row_id[:left] < left - 8 * k)
            out_ref[pl.ds(pl.multiple_of(done + 8 * k, 8), 8), :] = rows
            gram = pltpu.roll(jnp.concatenate([gram[8:], gram[:8]], axis=0), size - 8, 1)
            return gram, jnp.concatenate([inverse[8:], inverse[:8]], axis=0)

        gram, inverse = lax.fori_loop(0, panels, panel, (gram[:left], inverse[:left]))
        done += 8 * panels
        gram, inverse = gram[: size - done], inverse[: size - done]


def write_halves(state_ref, value, keep_ref, give_ref):
    half = value.shape[0] // 2
    cut = half // 2
    first = jnp.concatenate([value[:half, :half], value[half : half + cut, :half]], axis=0)
    second = jnp.concatenate([value[half + cut :, :half], value[half:, half:]], axis=0)
    mine = state_ref[2] == 0
    keep = jnp.where(mine, first, second)
    give = jnp.where(mine, second, first)
    keep_ref[...] = keep
    give_ref[...] = give


def read_halves(state_ref, own_ref, other_ref):
    own, other = own_ref[...], other_ref[...]
    mine = state_ref[2] == 0
    first = jnp.where(mine, own, other)
    second = jnp.where(mine, other, own)
    half = own.shape[1]
    cut = half // 2
    cross = jnp.concatenate([first[half:], second[:cut]], axis=0)
    return first[:half], cross, second[cut:]


def whole(blocks):
    first, cross, second = blocks
    return jnp.concatenate(
        [jnp.concatenate([first, cross.T], axis=1), jnp.concatenate([cross, second], axis=1)],
        axis=0,
    )


def half_dims(rank):
    return [(3 * rank // 4, rank // 2)] * 2


def gram_body(state_ref, core_ref, keep_ref, give_ref, acc_ref):
    step = pl.program_id(0)

    @pl.when(state_ref[0] == 1)
    def _():
        @pl.when(step == 0)
        def _():
            acc_ref[...] = jnp.zeros_like(acc_ref)

        rank, modes, width = core_ref.shape
        high, low = split(core_ref[...].reshape(rank * modes, width))
        acc_ref[...] += contract(high, jnp.concatenate([high, low], axis=1), 0, 0)

        @pl.when(step == pl.num_programs(0) - 1)
        def _():
            cross = acc_ref[:, width:]
            total = acc_ref[:, :width] + (cross + cross.T)
            write_halves(state_ref, total, keep_ref, give_ref)


def core_spec(rank, modes, width):
    return pl.BlockSpec((rank, modes, width), lambda s, state: (0, s * state[0], 0))


def gram(state, core):
    rank, mode_count, width = core.shape
    modes = min(16, mode_count)
    return pl.pallas_call(
        gram_body,
        grid_spec=pltpu.PrefetchScalarGridSpec(
            num_scalar_prefetch=1,
            grid=(mode_count // modes,),
            in_specs=[core_spec(rank, modes, width)],
            out_specs=[fixed(*dims) for dims in half_dims(width)],
            scratch_shapes=[pltpu.VMEM((width, 2 * width), F32)],
        ),
        out_shape=[shape(dims) for dims in half_dims(width)],
        name="gram",
    )(state, core)


def write_factor(state_ref, own_ref, other_ref, low_ref, inv_ref, work_ref):
    half = low_ref.shape[0] // 2
    first, cross, second = read_halves(state_ref, own_ref, other_ref)
    low_ref[:half, :half] = first
    low_ref[half:, :half] = cross
    low_ref[half:, half:] = second
    low_ref[:half, half:] = jnp.zeros((half, half), F32)
    inv_ref[:half, half:] = jnp.zeros((half, half), F32)

    def block(k, _):
        here = pl.ds(pl.multiple_of(k * half, half), half)
        diagonal = jnp.where(k == 0, low_ref[:half, :half], low_ref[half:, half:])
        inverse_factor(diagonal, work_ref)
        inverse = work_ref[...]
        inv_ref[here, :half] = inverse
        lower = exact(diagonal, inverse, 1, 1)

        @pl.when(k == 0)
        def _():
            low_ref[:half, :half] = lower
            low_cross = exact(low_ref[half:, :half], inverse, 1, 1)
            low_ref[half:, :half] = low_cross
            low_ref[half:, half:] -= exact(low_cross, low_cross, 1, 1)

        @pl.when(k == 1)
        def _():
            low_ref[half:, half:] = lower
            inv_ref[half:, half:] = inverse
            across = exact(low_ref[half:, :half], inv_ref[:half, :half], 1, 0)
            inv_ref[half:, :half] = -exact(inverse, across, 1, 0)

        return 0

    lax.fori_loop(0, 2, block, 0)


def absorbed_body(
    state_ref,
    own_ref,
    other_ref,
    core_ref,
    keep_ref,
    give_ref,
    low_ref,
    inv_ref,
    both_ref,
    acc_ref,
    mid_ref,
    work_ref,
):
    step = pl.program_id(0)

    @pl.when((state_ref[0] == 0) & (step == 0))
    def _():
        write_factor(state_ref, own_ref, other_ref, low_ref, inv_ref, work_ref)

    @pl.when(state_ref[0] == 1)
    def _():
        rank, modes, width = core_ref.shape

        @pl.when(step == 0)
        def _():
            acc_ref[...] = jnp.zeros_like(acc_ref)
            outer_high, outer_low = split(whole(read_halves(state_ref, own_ref, other_ref)))
            both_ref[:rank] = outer_high
            both_ref[rank:] = outer_low

        high, low = split(core_ref[...].transpose(1, 0, 2))
        both = both_ref[...]
        for i in range(modes):
            stacked = contract(both, high[i], 1, 0)
            rest = contract(both[:rank], low[i], 1, 0)
            main = stacked[:rank] + stacked[rank:]
            main_high = main.astype(BF16)
            mid_ref[i * rank : (i + 1) * rank, :width] = main_high
            mid_ref[i * rank : (i + 1) * rank, width:] = (
                (main - main_high.astype(F32)) * 0.5 + rest
            ).astype(BF16)
        acc_ref[...] += contract(high.reshape(modes * rank, width), mid_ref[...], 0, 0)

        @pl.when(step == pl.num_programs(0) - 1)
        def _():
            half = acc_ref[:, :width] * 0.5 + acc_ref[:, width:]
            write_halves(state_ref, half + half.T, keep_ref, give_ref)


def absorbed_gram(state, outer, core):
    rank, mode_count, width = core.shape
    modes = min(8, mode_count)
    return pl.pallas_call(
        absorbed_body,
        grid_spec=pltpu.PrefetchScalarGridSpec(
            num_scalar_prefetch=1,
            grid=(mode_count // modes,),
            in_specs=[fixed(*dims) for dims in half_dims(rank)] + [core_spec(rank, modes, width)],
            out_specs=[fixed(*dims) for dims in half_dims(width)] + [fixed(rank, rank)] * 2,
            scratch_shapes=[
                pltpu.VMEM((2 * rank, rank), BF16),
                pltpu.VMEM((width, 2 * width), F32),
                pltpu.VMEM((modes * rank, 2 * width), BF16),
                pltpu.VMEM((rank // 2, rank // 2), F32),
            ],
        ),
        out_shape=[shape(dims) for dims in half_dims(width)] + [shape((rank, rank))] * 2,
        name="absorbed_gram",
    )(state, *outer, core)


def project_step(state_ref, core_ref, map_ref, high_ref, low_ref, half_refs, both_ref, acc_ref):
    step = pl.program_id(0)
    rank, modes, width = core_ref.shape
    kept = map_ref.shape[1]

    @pl.when(step == 0)
    def _():
        acc_ref[...] = jnp.zeros_like(acc_ref)
        map_high, map_low = split(map_ref[...])
        both_ref[:, :kept] = map_high
        both_ref[:, kept:] = map_low

    high, low = split(core_ref[...].reshape(rank * modes, width))
    both = both_ref[...]
    first = contract(high, both, 1, 0)
    second = contract(low, both, 1, 0)
    mixed = first[:, :kept] + (first[:, kept:] + second[:, :kept])
    mixed = mixed.reshape(rank, modes, kept).transpose(1, 0, 2)
    mixed = jnp.concatenate([mixed[i] for i in range(modes)], axis=1)
    mixed_high, mixed_low = split(mixed)
    high_ref[...] = mixed_high
    low_ref[...] = mixed_low
    acc_ref[...] += contract(mixed_high, jnp.concatenate([mixed_high, mixed_low], axis=0), 1, 1)

    @pl.when(step == pl.num_programs(0) - 1)
    def _():
        cross = acc_ref[:, rank:]
        total = acc_ref[:, :rank] + (cross + cross.T)
        write_halves(state_ref, total, *half_refs)


def shaped_piece(front_ref, high_ref, low_ref):
    kept = front_ref.shape[1]
    front_high, front_low = split(front_ref[...].T)
    both = jnp.concatenate([front_high, front_low], axis=0)
    first = contract(both, high_ref[...], 1, 0)
    second = contract(front_high, low_ref[...], 1, 0)
    return first[:kept] + (first[kept:] + second)


def project_body(pieces, halves, state_ref, *refs):
    core_ref, map_ref, refs = refs[0], refs[1], refs[2:]
    if pieces:
        other_refs, refs = refs[:3], refs[3:]
        piece_refs, slots_ref, copied = refs[2 + halves : 2 + halves + pieces], refs[-2], refs[-1]
    high_ref, low_ref, half_refs = refs[0], refs[1], refs[2 : 2 + halves]
    both_ref, acc_ref = refs[2 + halves + pieces : 4 + halves + pieces]

    @pl.when(state_ref[0] == 1)
    def _():
        project_step(
            state_ref, core_ref, map_ref, high_ref, low_ref, half_refs, both_ref, acc_ref
        )

    if pieces:

        @pl.when(state_ref[0] == 0)
        def _():
            step = pl.program_id(0)
            slots_ref[step] = shaped_piece(*other_refs)
            copies = [
                pltpu.make_async_copy(slots_ref.at[d], piece_refs[d], copied.at[d])
                for d in range(pieces)
            ]
            for d in range(pieces):

                @pl.when(step == d)
                def _(d=d):
                    copies[d].start()

            @pl.when(step == pieces - 1)
            def _():
                for copy in copies:
                    copy.wait()


def project(state, core, right_map, other=None, pieces=0):
    rank, mode_count, width = core.shape
    kept = right_map.shape[1]
    modes = mode_count // pieces if pieces else min(16, mode_count)
    wide = pl.BlockSpec((rank, modes * kept), lambda s, state: (0, s * state[0]))
    in_specs = [core_spec(rank, modes, width), fixed(width, kept)]
    half_shapes = half_dims(rank)
    out_specs = [wide, wide] + [fixed(*dims) for dims in half_shapes]
    out_shape = [shape((rank, mode_count * kept), BF16)] * 2 + [shape(d) for d in half_shapes]
    scratch = [pltpu.VMEM((width, 2 * kept), BF16), pltpu.VMEM((rank, 2 * rank), F32)]
    operands = [core, right_map]
    if pieces:
        away = pl.BlockSpec(
            (rank, modes * kept), lambda s, state: (0, state[1] ^ (s * (1 - state[0])))
        )
        in_specs += [fixed(rank, kept), away, away]
        operands += other
        out_specs += [pl.BlockSpec(memory_space=pl.ANY)] * pieces
        out_shape += [shape((kept, modes * kept))] * pieces
        scratch += [
            pltpu.VMEM((pieces, kept, modes * kept), F32),
            pltpu.SemaphoreType.DMA((pieces,)),
        ]
    return pl.pallas_call(
        functools.partial(project_body, pieces, len(half_shapes)),
        grid_spec=pltpu.PrefetchScalarGridSpec(
            num_scalar_prefetch=1,
            grid=(mode_count // modes,),
            in_specs=in_specs,
            out_specs=out_specs,
            scratch_shapes=scratch,
        ),
        out_shape=out_shape,
        name="project",
    )(state, *operands)


SMEM = pl.BlockSpec(memory_space=pltpu.SMEM)
VMEM = pl.BlockSpec(memory_space=pltpu.VMEM)
ANY = pl.BlockSpec(memory_space=pl.ANY)


def basis_body(
    state_ref,
    own_ref,
    other_ref,
    sketch_ref,
    low_any,
    inv_any,
    basis_ref,
    front_ref,
    map_ref,
    work_ref,
    total_ref,
    low_ref,
    inv_ref,
    copied,
):
    absorbed = state_ref[4] == 1

    @pl.when(state_ref[0] == 1)
    def _():
        copies = [
            pltpu.make_async_copy(low_any, low_ref, copied.at[0]),
            pltpu.make_async_copy(inv_any, inv_ref, copied.at[1]),
        ]

        @pl.when(absorbed)
        def _():
            for copy in copies:
                copy.start()

        total_ref[...] = whole(read_halves(state_ref, own_ref, other_ref))

        @pl.when(absorbed)
        def _():
            for copy in copies:
                copy.wait()
            lower = low_ref[...]
            total_ref[...] = exact(exact(lower, total_ref[...], 0, 0), lower, 1, 0)

        total = total_ref[...]
        powered = exact(total, exact(total, sketch_ref[...], 1, 0), 1, 0)
        inverse_factor(exact(powered, powered, 0, 0), work_ref)
        frame = exact(powered, work_ref[...], 1, 1)
        basis_ref[...] = frame

        @pl.when(absorbed)
        def _():
            front_ref[...] = exact(low_ref[...], frame, 1, 0)
            map_ref[...] = exact(inv_ref[...], frame, 0, 0)


def basis(state, halves, sketch, lower, inverse):
    rank, kept = sketch.shape
    return pl.pallas_call(
        basis_body,
        in_specs=[SMEM] + [VMEM] * 3 + [ANY] * 2,
        out_shape=[shape(sketch.shape)] * 3,
        scratch_shapes=[
            pltpu.VMEM((kept, kept), F32),
            pltpu.VMEM((rank, rank), F32),
            pltpu.VMEM((rank, rank), F32),
            pltpu.VMEM((rank, rank), F32),
            pltpu.SemaphoreType.DMA((2,)),
        ],
        name="basis",
    )(state, *halves, sketch, lower, inverse)


def piece_body(state_ref, front_ref, high_ref, low_ref, piece_ref):
    @pl.when(state_ref[0] == 1)
    def _():
        piece_ref[...] = shaped_piece(front_ref, high_ref, low_ref)


def round_piece(state, front, high, low, pieces):
    rank, wide = high.shape
    kept = front.shape[1]
    width = wide // pieces
    parts = 2 if width % 2048 == 0 else 1
    block = pl.BlockSpec(
        (rank, width // parts), lambda s, state: (0, (state[1] * parts + s) * state[0])
    )
    return pl.pallas_call(
        piece_body,
        grid_spec=pltpu.PrefetchScalarGridSpec(
            num_scalar_prefetch=1,
            grid=(parts,),
            in_specs=[fixed(rank, kept), block, block],
            out_specs=pl.BlockSpec((kept, width // parts), lambda s, state: (0, s * state[0])),
        ),
        out_shape=shape((kept, width)),
        name="round_piece",
    )(state, front, high, low)


def layout_body(pieces, scale, state_ref, *refs):
    sides, (out_ref, slots_ref, laid_ref, taken, placed) = (
        (refs[:pieces], refs[pieces : 2 * pieces]),
        refs[2 * pieces :],
    )
    vec = state_ref[1]
    for side in (0, 1):

        @pl.when(state_ref[2] == side)
        def _(side=side):
            copies = [
                pltpu.make_async_copy(sides[side][d], slots_ref.at[d], taken.at[d])
                for d in range(pieces)
            ]
            for copy in copies:
                copy.start()
            for copy in copies:
                copy.wait()

    kept, modes = laid_ref.shape[1:3]
    copies = []
    for d in range(pieces):
        stacked = jnp.stack(
            [slots_ref[d, :, i * kept : (i + 1) * kept] for i in range(modes)], axis=0
        )
        laid_ref[d] = stacked.transpose(1, 0, 2) * scale
        copies.append(pltpu.make_async_copy(laid_ref.at[d], out_ref.at[:, vec ^ d], placed.at[d]))
        copies[-1].start()
    for copy in copies:
        copy.wait()


def lay_out(state, first, last, scale):
    pieces = len(first)
    kept, width = first[0].shape
    modes = width // kept
    anywhere = pl.BlockSpec(memory_space=pl.ANY)
    return pl.pallas_call(
        functools.partial(layout_body, pieces, scale),
        in_specs=[SMEM] + [anywhere] * (2 * pieces),
        out_specs=anywhere,
        out_shape=shape((kept, pieces, modes, kept)),
        scratch_shapes=[
            pltpu.VMEM((pieces, kept, width), F32),
            pltpu.VMEM((pieces, kept, modes, kept), F32),
            pltpu.SemaphoreType.DMA((pieces,)),
            pltpu.SemaphoreType.DMA((pieces,)),
        ],
        name="lay_out",
    )(state, *first, *last)


def pair_list(count):
    return [(p, q) for p in range(count) for q in range(p, count)]


def chunk_rows(state_ref, half, d, chunks, kept):
    size = kept // (2 * chunks)
    start = (half * chunks + (state_ref[3] ^ d)) * size
    return (pl.multiple_of(start, 8) if size % 8 == 0 else start), size


def halves_of(state_ref, own_ref, other_ref):
    return (own_ref, state_ref[2]), (other_ref, 1 - state_ref[2])


def place_chunks(state_ref, own_ref, other_ref, out_ref):
    chunks, rows, kept = own_ref.shape
    for d in range(chunks):
        for ref, half in halves_of(state_ref, own_ref, other_ref):
            start, size = chunk_rows(state_ref, half, d, chunks, kept)
            for i in range(rows // size):
                out_ref[pl.ds(i * kept + start, size), :] = ref[d, i * size : (i + 1) * size, :]


def margin_body(count, state_ref, *refs):
    piece_refs, frame_anys, refs = refs[:count], refs[count : 2 * count], refs[2 * count :]
    own_any, other_any, _, keep_ref, give_ref, stage_ref, env_ref, out_ref = refs[:8]
    frame_ref, env_own_ref, env_other_ref, env_in_ref, copied = refs[8:]
    step = pl.program_id(0)
    pairs = pair_list(count)
    index_of = {pair: i for i, pair in enumerate(pairs)}

    @pl.when(state_ref[0] == 1)
    def _():
        me = state_ref[1]
        kept = piece_refs[0].shape[0]

        @pl.when(step == 0)
        def _():
            out_ref[...] = jnp.zeros_like(out_ref)

            @pl.when(state_ref[4] == 0)
            def _():
                copies = [
                    pltpu.make_async_copy(frame_anys[d], frame_ref.at[me ^ d], copied.at[d])
                    for d in range(count)
                ]
                for copy in copies:
                    copy.start()
                for copy in copies:
                    copy.wait()
                for i, (p, q) in enumerate(pairs):
                    env_in_ref[i * kept : (i + 1) * kept] = exact(frame_ref[p], frame_ref[q], 0, 0)

            @pl.when(state_ref[4] == 1)
            def _():
                copies = [
                    pltpu.make_async_copy(own_any, env_own_ref, copied.at[0]),
                    pltpu.make_async_copy(other_any, env_other_ref, copied.at[1]),
                ]
                for copy in copies:
                    copy.start()
                for copy in copies:
                    copy.wait()
                place_chunks(state_ref, env_own_ref, env_other_ref, env_in_ref)

            for i, (p, q) in enumerate(pairs):
                env = env_in_ref[i * kept : (i + 1) * kept]
                env_high, env_low = split(env)
                env_ref[q, p * kept : (p + 1) * kept] = env_high
                env_ref[q, (count + p) * kept : (count + p + 1) * kept] = env_low

        for d in range(count):
            stage_ref[me ^ d] = piece_refs[d][...]
        modes = piece_refs[0].shape[1] // kept

        def tall(value):
            return jnp.concatenate(
                [value[:, i * kept : (i + 1) * kept] for i in range(modes)], axis=0
            )

        highs, lows, carried = [], [], {}
        for q in range(count):
            high, low = split(stage_ref[q])
            highs.append(tall(high))
            lows.append(tall(low))
            rows = (q + 1) * kept
            env_high = env_ref[q, :rows]
            env_low = env_ref[q, count * kept : count * kept + rows]
            stacked = contract(jnp.concatenate([env_high, env_low], axis=0), high, 1, 0)
            moved = stacked[:rows] + (stacked[rows:] + contract(env_high, low, 1, 0))
            for p in range(q + 1):
                carried[p, q] = split(tall(moved[p * kept : (p + 1) * kept]))
        for p in range(count):
            partners = range(p, count)
            main = contract(
                jnp.concatenate([highs[p], lows[p]], axis=1),
                jnp.concatenate([carried[p, q][0] for q in partners], axis=1),
                0,
                0,
            )
            cross = contract(
                highs[p], jnp.concatenate([carried[p, q][1] for q in partners], axis=1), 0, 0
            )
            total = main[:kept] + (main[kept:] + cross)
            for j, q in enumerate(partners):
                i = index_of[p, q]
                out_ref[i * kept : (i + 1) * kept] += total[:, j * kept : (j + 1) * kept]

        @pl.when(step == pl.num_programs(0) - 1)
        def _():
            chunks, rows = keep_ref.shape[:2]
            for d in range(chunks):
                for ref, half in halves_of(state_ref, keep_ref, give_ref):
                    start, size = chunk_rows(state_ref, half, d, chunks, kept)
                    for i in range(rows // size):
                        ref[d, i * size : (i + 1) * size, :] = out_ref[
                            pl.ds(i * kept + start, size), :
                        ]


def margin_terms(state, pieces, frames, env, token):
    count = len(pieces)
    kept, wide = pieces[0].shape
    chunk = min(4 * kept, wide)
    total = count * (count + 1) // 2 * kept
    piece_spec = pl.BlockSpec((kept, chunk), lambda s, state: (0, s * state[0]))
    part = env[0].shape
    scratch = [
        pltpu.VMEM((count, kept, chunk), F32),
        pltpu.VMEM((count, 2 * count * kept, kept), BF16),
        pltpu.VMEM((total, kept), F32),
        pltpu.VMEM((count, *frames[0].shape), F32),
        pltpu.VMEM(part, F32),
        pltpu.VMEM(part, F32),
        pltpu.VMEM((total, kept), F32),
        pltpu.SemaphoreType.DMA((count,)),
    ]
    return pl.pallas_call(
        functools.partial(margin_body, count),
        grid_spec=pltpu.PrefetchScalarGridSpec(
            num_scalar_prefetch=1,
            grid=(wide // chunk,),
            in_specs=[piece_spec] * count + [ANY] * (count + 3),
            out_specs=[fixed(*part)] * 2,
            scratch_shapes=scratch,
        ),
        out_shape=[shape(part)] * 2,
        name="margin_terms",
    )(state, *pieces, *frames, *env, token)


def unset(dims):
    return pl.pallas_call(
        lambda ref: None, out_specs=ANY, out_shape=shape(dims), name="unset"
    )()


def pair_index(count, first, second):
    low, high = jnp.minimum(first, second), jnp.maximum(first, second)
    return low * count - low * (low - 1) // 2 + high - low


def owner_body(count, state_ref, *refs):
    part_refs, (out_ref, sum_ref) = refs[:-2], refs[-2:]
    sum_ref[...] = tree_sum([ref[...] for ref in part_refs])
    size = sum_ref.shape[0] // (count * (count + 1) // 2)
    for d in range(count):
        for q in range(count):
            start = pair_index(count, state_ref[1] ^ d, q) * size
            if size % 8 == 0:
                start = pl.multiple_of(start, 8)
            out_ref[d, q * size : (q + 1) * size, :] = sum_ref[pl.ds(start, size), :]


def owner_rows(state, parts, count):
    rows, kept = parts[0].shape
    size = rows // (count * (count + 1) // 2)
    return pl.pallas_call(
        functools.partial(owner_body, count),
        in_specs=[SMEM] + [VMEM] * len(parts),
        out_shape=shape((count, count * size, kept)),
        scratch_shapes=[pltpu.VMEM((rows, kept), F32)],
        name="owner_rows",
    )(state, *parts)


def pick_body(count, state_ref, own_ref, other_ref, own_row_ref, other_row_ref, out_ref, env_ref):
    kept = out_ref.shape[0]
    me = state_ref[1]

    @pl.when(state_ref[2] == 0)
    def _():
        place_chunks(state_ref, own_ref, other_ref, env_ref)
        for q in range(count):
            start = pl.multiple_of(pair_index(count, me, q) * kept, kept)
            block = env_ref[pl.ds(start, kept), :]
            out_ref[:, q * kept : (q + 1) * kept] = jnp.where(me > q, block.T, block)

    @pl.when(state_ref[2] == 1)
    def _():
        place_chunks(state_ref, own_row_ref, other_row_ref, env_ref)
        for q in range(count):
            block = env_ref[q * kept : (q + 1) * kept, :]
            out_ref[:, q * kept : (q + 1) * kept] = jnp.where(me > q, block.T, block)


def pick(state, env_first, env_last, count):
    kept = env_first[0].shape[2]
    return pl.pallas_call(
        functools.partial(pick_body, count),
        in_specs=[SMEM] + [VMEM] * 4,
        out_shape=shape((kept, count * kept)),
        scratch_shapes=[pltpu.VMEM((count * (count + 1) // 2 * kept, kept), F32)],
        name="pick",
    )(state, *env_first, *env_last)


def send(block, axis, size, distance):
    return lax.ppermute(block, axis, [(i, i ^ distance) for i in range(size)])


def swap(block):
    return send(block, "cores", 2, 1)


def send_from(block, side, size, distance):
    pairs = [(side * size + i, side * size + (i ^ distance)) for i in range(size)]
    return lax.ppermute(block, ("cores", "vec"), pairs)


def exchange_sum(block, axis, size):
    return tree_sum([block] + [send(block, axis, size, d) for d in range(1, size)])


def local(train_cores, sketch, exit_sketch):
    core = train_cores[0]
    rank, mode_count, _ = core.shape
    kept = sketch.shape[1]
    row_size = lax.axis_size("row")
    vec_size = lax.axis_size("vec")
    side = lax.axis_index("cores")
    row = lax.axis_index("row")
    vec = lax.axis_index("vec")
    first_side = (side == 0).astype(jnp.int32)
    place = [vec, side, row]
    state_first = jnp.stack([first_side, *place, jnp.int32(0)])
    state_last = jnp.stack([1 - first_side, *place, jnp.int32(0)])
    state_next = jnp.stack([1 - first_side, *place, jnp.int32(1)])
    state_both = jnp.stack([jnp.int32(1), *place, jnp.int32(1)])
    scale = math.sqrt(kept * MODE)

    def row_total(keep, give, holder):
        mine = jnp.where(side == holder, keep, swap(give))
        own = exchange_sum(mine, "row", row_size)
        return own, swap(own)

    def row_parts(keep, give, holder):
        mine = jnp.where(side == holder, keep, swap(give))
        return [mine[0]] + [send(mine[d], "row", row_size, d) for d in range(1, row_size)]

    def row_collect(chunk):
        own = jnp.stack([chunk] + [send(chunk, "row", row_size, d) for d in range(1, row_size)])
        return own, swap(own)

    def env_total(keep, give, holder):
        return row_collect(exchange_sum(tree_sum(row_parts(keep, give, holder)), "vec", vec_size))

    def env_rows(keep, give, holder):
        rows = owner_rows(state_both, row_parts(keep, give, holder), vec_size)
        parts = [rows[0]] + [send(rows[d], "vec", vec_size, d) for d in range(1, vec_size)]
        return row_collect(tree_sum(parts))

    def at(state, d):
        return state.at[1].set(vec ^ d)

    def sent(pieces, holder, distances):
        for d in distances:
            pieces[d] = send_from(pieces[d], holder, vec_size, d)

    late = [vec_size // 2]
    pair_count = vec_size * (vec_size + 1) // 2
    blank = unset((row_size, pair_count * kept // (2 * row_size), kept))
    gram_first = row_total(*gram(state_first, core), 0)
    *gram_last, lower_own, inverse_own = absorbed_gram(state_last, gram_first, core)
    gram_last = row_total(*gram_last, 1)
    lower = jnp.where(side == 0, lower_own, swap(lower_own))
    inverse = jnp.where(side == 0, inverse_own, swap(inverse_own))
    exit_frame, _, _ = basis(state_last, gram_last, exit_sketch, lower_own, inverse_own)
    last_high, last_low, *left_last = project(state_last, core, exit_frame)
    left_last = row_total(*left_last, 1)
    other_sketch = swap(sketch)
    frame_last, front, map_first = basis(
        state_both, left_last, jnp.where(side == 1, sketch, other_sketch), lower, inverse
    )
    rounded_last = [front, last_high, last_low]
    if mode_count // vec_size % 8 == 0:
        first_high, first_low, *rest = project(
            state_first, core, map_first, rounded_last, vec_size
        )
        left_first, own_last = rest[:2], rest[2:]
    else:
        first_high, first_low, *left_first = project(state_first, core, map_first)
        own_last = [
            round_piece(at(state_last, d), *rounded_last, vec_size) for d in range(vec_size)
        ]
    left_first = row_total(*left_first, 0)
    *own_last, left_own, left_other = lax.optimization_barrier((*own_last, *left_first))
    left_first = (left_own, left_other)
    pieces_last = list(own_last)
    sent(pieces_last, 1, [d for d in range(1, vec_size) if d not in late])
    frame_first, _, _ = basis(state_first, left_first, sketch, lower, inverse)
    own_first = [None] * vec_size
    for d in range(vec_size - 1, -1, -1):
        own_first[d] = round_piece(at(state_first, d), frame_first, first_high, first_low, vec_size)
    pieces_first = list(own_first)
    sent(pieces_first, 0, range(1, vec_size))
    rounded = lay_out(state_both, own_first, own_last, scale)
    frames = [frame_first] + [send_from(frame_first, 0, vec_size, d) for d in range(1, vec_size)]
    held = [pieces_last[d] for d in late]
    token = swap(pieces_first[late[0]][:8, :128])
    for d, piece in zip(late, held):
        pieces_last[d] = piece
    sent(pieces_last, 1, late)
    env_first = margin_terms(state_first, pieces_first, frames, (blank, blank), token)
    env_first = env_total(*env_first, 0)
    env_last = env_rows(*margin_terms(state_next, pieces_last, frames, env_first, token), 1)
    margins = pick(state_both, env_first, env_last, vec_size)
    bases = jnp.where(side == 0, frame_first, frame_last) * math.sqrt(rank)
    return rounded.reshape(1, kept, mode_count, kept), bases[None], margins[None]


def solution(mesh):
    return jax.shard_map(
        local,
        mesh=mesh,
        in_specs=(P("vec", "cores", "row", None), P("cores", None), P()),
        out_specs=(
            P("vec", "cores", "row", None),
            P("vec", "cores", None),
            P("vec", "cores", None),
        ),
        check_vma=False,
    )
```

```python
import functools
import math

import jax
import jax.numpy as jnp
from jax import lax
from jax.experimental import pallas as pl
from jax.experimental.pallas import tpu as pltpu
from jax.sharding import PartitionSpec as P


MODE = 256
F32 = jnp.float32
BF16 = jnp.bfloat16


def contract(left, right, left_dim, right_dim, precision=None):
    return lax.dot_general(
        left,
        right,
        (((left_dim,), (right_dim,)), ((), ())),
        precision=precision,
        preferred_element_type=F32,
    )


exact = functools.partial(contract, precision=lax.Precision.HIGHEST)


def split(value):
    high = value.astype(BF16)
    return high, (value - high.astype(F32)).astype(BF16)


def room(mebibytes):
    return pltpu.CompilerParams(vmem_limit_bytes=mebibytes << 20)


def tree_sum(terms):
    terms = list(terms)
    while len(terms) > 1:
        terms = [terms[i] + terms[i + 1] for i in range(0, len(terms), 2)]
    return terms[0]


def shape(dims, dtype=F32):
    return jax.ShapeDtypeStruct(dims, dtype)


def fixed(*dims):
    return pl.BlockSpec(dims, lambda *_: (0,) * len(dims))


def inverse_factor(gram, out_ref, unrolled=False):
    size = gram.shape[0]
    row_id = lax.broadcasted_iota(jnp.int32, (size, size), 0)
    col_id = lax.broadcasted_iota(jnp.int32, (size, size), 1)
    inverse = jnp.where(row_id == col_id, 1.0, 0.0).astype(F32)

    def eliminate(gram, inverse, column, open_rows):
        left = gram.shape[0]
        rows = row_id[:left]
        columns = [
            jnp.broadcast_to(gram[:, column + t : column + t + 1], (left, size)) for t in range(8)
        ]
        scale = jnp.zeros((8, size), F32)
        for t in range(8):
            pivot = columns[t][t : t + 1, :]
            use = rows > t
            if open_rows is not None:
                use = use & open_rows
            factor = jnp.where(use, columns[t] * (1.0 / pivot), 0.0)
            for s in range(t + 1, 8):
                columns[s] = columns[s] - factor * columns[s][t : t + 1, :]
            gram = gram - factor * gram[t : t + 1, :]
            inverse = inverse - factor * inverse[t : t + 1, :]
            scale = jnp.where(rows[:8] == t, lax.rsqrt(pivot), scale)
        return gram, inverse, inverse[:8] * scale

    if unrolled:
        for start in range(0, size, 8):
            gram, inverse, rows = eliminate(gram, inverse, start, None)
            out_ref[start : start + 8, :] = rows
            gram, inverse = gram[8:], inverse[8:]
        return

    done = 0
    while done < size:
        left = size - done
        panels = left // 16 if left > 16 else left // 8

        def panel(k, carry, left=left, done=done):
            gram, inverse = carry
            gram, inverse, rows = eliminate(gram, inverse, 0, row_id[:left] < left - 8 * k)
            out_ref[pl.ds(pl.multiple_of(done + 8 * k, 8), 8), :] = rows
            gram = pltpu.roll(jnp.concatenate([gram[8:], gram[:8]], axis=0), size - 8, 1)
            return gram, jnp.concatenate([inverse[8:], inverse[:8]], axis=0)

        gram, inverse = lax.fori_loop(0, panels, panel, (gram[:left], inverse[:left]))
        done += 8 * panels
        gram, inverse = gram[: size - done], inverse[: size - done]


def write_halves(state_ref, value, keep_ref, give_ref):
    half = value.shape[0] // 2
    cut = half // 2
    first = jnp.concatenate([value[:half, :half], value[half : half + cut, :half]], axis=0)
    second = jnp.concatenate([value[half + cut :, :half], value[half:, half:]], axis=0)
    mine = state_ref[2] == 0
    keep = jnp.where(mine, first, second)
    give = jnp.where(mine, second, first)
    keep_ref[...] = keep
    give_ref[...] = give


def read_halves(state_ref, own_ref, other_ref):
    own, other = own_ref[...], other_ref[...]
    mine = state_ref[2] == 0
    first = jnp.where(mine, own, other)
    second = jnp.where(mine, other, own)
    half = own.shape[1]
    cut = half // 2
    cross = jnp.concatenate([first[half:], second[:cut]], axis=0)
    return first[:half], cross, second[cut:]


def whole(blocks):
    first, cross, second = blocks
    return jnp.concatenate(
        [jnp.concatenate([first, cross.T], axis=1), jnp.concatenate([cross, second], axis=1)],
        axis=0,
    )


def half_dims(rank):
    return [(3 * rank // 4, rank // 2)] * 2


def gram_body(state_ref, core_ref, keep_ref, give_ref, acc_ref):
    step = pl.program_id(0)

    @pl.when(state_ref[0] == 1)
    def _():
        @pl.when(step == 0)
        def _():
            acc_ref[...] = jnp.zeros_like(acc_ref)

        rank, modes, width = core_ref.shape
        high, low = split(core_ref[...].reshape(rank * modes, width))
        acc_ref[...] += contract(high, jnp.concatenate([high, low], axis=1), 0, 0)

        @pl.when(step == pl.num_programs(0) - 1)
        def _():
            cross = acc_ref[:, width:]
            total = acc_ref[:, :width] + (cross + cross.T)
            write_halves(state_ref, total, keep_ref, give_ref)


def core_spec(rank, modes, width):
    return pl.BlockSpec((rank, modes, width), lambda s, state: (0, s * state[0], 0))


def gram(state, core):
    rank, mode_count, width = core.shape
    modes = min(16, mode_count)
    return pl.pallas_call(
        gram_body,
        grid_spec=pltpu.PrefetchScalarGridSpec(
            num_scalar_prefetch=1,
            grid=(mode_count // modes,),
            in_specs=[core_spec(rank, modes, width)],
            out_specs=[fixed(*dims) for dims in half_dims(width)],
            scratch_shapes=[pltpu.VMEM((width, 2 * width), F32)],
        ),
        out_shape=[shape(dims) for dims in half_dims(width)],
        name="gram",
        compiler_params=room(24),
    )(state, core)


def write_factor(state_ref, own_ref, other_ref, low_ref, inv_ref, work_ref):
    half = low_ref.shape[0] // 2
    first, cross, second = read_halves(state_ref, own_ref, other_ref)
    low_ref[:half, :half] = first
    low_ref[half:, :half] = cross
    low_ref[half:, half:] = second
    low_ref[:half, half:] = jnp.zeros((half, half), F32)
    inv_ref[:half, half:] = jnp.zeros((half, half), F32)

    def block(k, _):
        here = pl.ds(pl.multiple_of(k * half, half), half)
        diagonal = jnp.where(k == 0, low_ref[:half, :half], low_ref[half:, half:])
        inverse_factor(diagonal, work_ref)
        inverse = work_ref[...]
        inv_ref[here, :half] = inverse
        lower = exact(diagonal, inverse, 1, 1)

        @pl.when(k == 0)
        def _():
            low_ref[:half, :half] = lower
            low_cross = exact(low_ref[half:, :half], inverse, 1, 1)
            low_ref[half:, :half] = low_cross
            low_ref[half:, half:] -= exact(low_cross, low_cross, 1, 1)

        @pl.when(k == 1)
        def _():
            low_ref[half:, half:] = lower
            inv_ref[half:, half:] = inverse
            across = exact(low_ref[half:, :half], inv_ref[:half, :half], 1, 0)
            inv_ref[half:, :half] = -exact(inverse, across, 1, 0)

        return 0

    lax.fori_loop(0, 2, block, 0)


def absorbed_body(
    state_ref,
    own_ref,
    other_ref,
    core_ref,
    keep_ref,
    give_ref,
    low_ref,
    inv_ref,
    both_ref,
    acc_ref,
    mid_ref,
    work_ref,
):
    step = pl.program_id(0)

    @pl.when((state_ref[0] == 0) & (step == 0))
    def _():
        write_factor(state_ref, own_ref, other_ref, low_ref, inv_ref, work_ref)

    @pl.when(state_ref[0] == 1)
    def _():
        rank, modes, width = core_ref.shape

        @pl.when(step == 0)
        def _():
            acc_ref[...] = jnp.zeros_like(acc_ref)
            outer_high, outer_low = split(whole(read_halves(state_ref, own_ref, other_ref)))
            both_ref[:rank] = outer_high
            both_ref[rank:] = outer_low

        high, low = split(core_ref[...].transpose(1, 0, 2))
        both = both_ref[...]
        for i in range(modes):
            stacked = contract(both, high[i], 1, 0)
            rest = contract(both[:rank], low[i], 1, 0)
            main = stacked[:rank] + stacked[rank:]
            main_high = main.astype(BF16)
            mid_ref[i * rank : (i + 1) * rank, :width] = main_high
            mid_ref[i * rank : (i + 1) * rank, width:] = (
                (main - main_high.astype(F32)) * 0.5 + rest
            ).astype(BF16)
        acc_ref[...] += contract(high.reshape(modes * rank, width), mid_ref[...], 0, 0)

        @pl.when(step == pl.num_programs(0) - 1)
        def _():
            half = acc_ref[:, :width] * 0.5 + acc_ref[:, width:]
            write_halves(state_ref, half + half.T, keep_ref, give_ref)


def absorbed_gram(state, outer, core):
    rank, mode_count, width = core.shape
    modes = min(8, mode_count)
    return pl.pallas_call(
        absorbed_body,
        grid_spec=pltpu.PrefetchScalarGridSpec(
            num_scalar_prefetch=1,
            grid=(mode_count // modes,),
            in_specs=[fixed(*dims) for dims in half_dims(rank)] + [core_spec(rank, modes, width)],
            out_specs=[fixed(*dims) for dims in half_dims(width)] + [fixed(rank, rank)] * 2,
            scratch_shapes=[
                pltpu.VMEM((2 * rank, rank), BF16),
                pltpu.VMEM((width, 2 * width), F32),
                pltpu.VMEM((modes * rank, 2 * width), BF16),
                pltpu.VMEM((rank // 2, rank // 2), F32),
            ],
        ),
        out_shape=[shape(dims) for dims in half_dims(width)] + [shape((rank, rank))] * 2,
        name="absorbed_gram",
        compiler_params=room(20),
    )(state, *outer, core)


def project_step(state_ref, core_ref, map_ref, high_ref, low_ref, half_refs, both_ref, acc_ref):
    step = pl.program_id(0)
    rank, modes, width = core_ref.shape
    kept = map_ref.shape[1]

    @pl.when(step == 0)
    def _():
        acc_ref[...] = jnp.zeros_like(acc_ref)
        map_high, map_low = split(map_ref[...])
        both_ref[:, :kept] = map_high
        both_ref[:, kept:] = map_low

    high, low = split(core_ref[...].reshape(rank * modes, width))
    both = both_ref[...]
    first = contract(high, both, 1, 0)
    second = contract(low, both, 1, 0)
    mixed = first[:, :kept] + (first[:, kept:] + second[:, :kept])
    mixed = mixed.reshape(rank, modes, kept).transpose(1, 0, 2)
    mixed = jnp.concatenate([mixed[i] for i in range(modes)], axis=1)
    mixed_high, mixed_low = split(mixed)
    high_ref[...] = mixed_high
    low_ref[...] = mixed_low
    acc_ref[...] += contract(mixed_high, jnp.concatenate([mixed_high, mixed_low], axis=0), 1, 1)

    @pl.when(step == pl.num_programs(0) - 1)
    def _():
        cross = acc_ref[:, rank:]
        total = acc_ref[:, :rank] + (cross + cross.T)
        write_halves(state_ref, total, *half_refs)


def shaped_piece(front_ref, high_ref, low_ref):
    kept = front_ref.shape[1]
    front_high, front_low = split(front_ref[...].T)
    both = jnp.concatenate([front_high, front_low], axis=0)
    first = contract(both, high_ref[...], 1, 0)
    second = contract(front_high, low_ref[...], 1, 0)
    return first[:kept] + (first[kept:] + second)


def project_body(pieces, halves, state_ref, *refs):
    core_ref, map_ref, refs = refs[0], refs[1], refs[2:]
    if pieces:
        other_refs, refs = refs[:3], refs[3:]
        piece_refs, slots_ref, copied = refs[2 + halves : 2 + halves + pieces], refs[-2], refs[-1]
    high_ref, low_ref, half_refs = refs[0], refs[1], refs[2 : 2 + halves]
    both_ref, acc_ref = refs[2 + halves + pieces : 4 + halves + pieces]

    @pl.when(state_ref[0] == 1)
    def _():
        project_step(
            state_ref, core_ref, map_ref, high_ref, low_ref, half_refs, both_ref, acc_ref
        )

    if pieces:

        @pl.when(state_ref[0] == 0)
        def _():
            step = pl.program_id(0)
            slots_ref[step] = shaped_piece(*other_refs)
            copies = [
                pltpu.make_async_copy(slots_ref.at[d], piece_refs[d], copied.at[d])
                for d in range(pieces)
            ]
            for d in range(pieces):

                @pl.when(step == d)
                def _(d=d):
                    copies[d].start()

            @pl.when(step == pieces - 1)
            def _():
                for copy in copies:
                    copy.wait()


def project(state, core, right_map, other=None, pieces=0):
    rank, mode_count, width = core.shape
    kept = right_map.shape[1]
    modes = mode_count // pieces if pieces else min(16, mode_count)
    wide = pl.BlockSpec((rank, modes * kept), lambda s, state: (0, s * state[0]))
    in_specs = [core_spec(rank, modes, width), fixed(width, kept)]
    half_shapes = half_dims(rank)
    out_specs = [wide, wide] + [fixed(*dims) for dims in half_shapes]
    out_shape = [shape((rank, mode_count * kept), BF16)] * 2 + [shape(d) for d in half_shapes]
    scratch = [pltpu.VMEM((width, 2 * kept), BF16), pltpu.VMEM((rank, 2 * rank), F32)]
    operands = [core, right_map]
    if pieces:
        out_shape[:2] = [pltpu.HBM((rank, mode_count * kept), BF16)] * 2
        away = pl.BlockSpec(
            (rank, modes * kept), lambda s, state: (0, state[1] ^ (s * (1 - state[0])))
        )
        in_specs += [fixed(rank, kept), away, away]
        operands += other
        out_specs += [pl.BlockSpec(memory_space=pl.ANY)] * pieces
        out_shape += [shape((kept, modes * kept))] * pieces
        scratch += [
            pltpu.VMEM((pieces, kept, modes * kept), F32),
            pltpu.SemaphoreType.DMA((pieces,)),
        ]
    return pl.pallas_call(
        functools.partial(project_body, pieces, len(half_shapes)),
        grid_spec=pltpu.PrefetchScalarGridSpec(
            num_scalar_prefetch=1,
            grid=(mode_count // modes,),
            in_specs=in_specs,
            out_specs=out_specs,
            scratch_shapes=scratch,
        ),
        out_shape=out_shape,
        name="project",
        compiler_params=room(30),
    )(state, *operands)


SMEM = pl.BlockSpec(memory_space=pltpu.SMEM)
VMEM = pl.BlockSpec(memory_space=pltpu.VMEM)
ANY = pl.BlockSpec(memory_space=pl.ANY)


def basis_body(
    state_ref,
    own_ref,
    other_ref,
    sketch_ref,
    low_any,
    inv_any,
    basis_ref,
    front_ref,
    map_ref,
    work_ref,
    total_ref,
    low_ref,
    inv_ref,
    copied,
):
    absorbed = state_ref[4] == 1

    @pl.when(state_ref[0] == 1)
    def _():
        copies = [
            pltpu.make_async_copy(low_any, low_ref, copied.at[0]),
            pltpu.make_async_copy(inv_any, inv_ref, copied.at[1]),
        ]

        @pl.when(absorbed)
        def _():
            for copy in copies:
                copy.start()

        total_ref[...] = whole(read_halves(state_ref, own_ref, other_ref))

        @pl.when(absorbed)
        def _():
            for copy in copies:
                copy.wait()
            lower = low_ref[...]
            total_ref[...] = exact(exact(lower, total_ref[...], 0, 0), lower, 1, 0)

        total = total_ref[...]
        powered = exact(total, exact(total, sketch_ref[...], 1, 0), 1, 0)
        inverse_factor(exact(powered, powered, 0, 0), work_ref)
        frame = exact(powered, work_ref[...], 1, 1)
        basis_ref[...] = frame

        @pl.when(absorbed)
        def _():
            front_ref[...] = exact(low_ref[...], frame, 1, 0)
            map_ref[...] = exact(inv_ref[...], frame, 0, 0)


def basis(state, halves, sketch, lower, inverse):
    rank, kept = sketch.shape
    return pl.pallas_call(
        basis_body,
        in_specs=[SMEM] + [VMEM] * 3 + [ANY] * 2,
        out_shape=[shape(sketch.shape)] * 3,
        scratch_shapes=[
            pltpu.VMEM((kept, kept), F32),
            pltpu.VMEM((rank, rank), F32),
            pltpu.VMEM((rank, rank), F32),
            pltpu.VMEM((rank, rank), F32),
            pltpu.SemaphoreType.DMA((2,)),
        ],
        name="basis",
        compiler_params=room(8),
    )(state, *halves, sketch, lower, inverse)


def piece_body(state_ref, front_ref, high_ref, low_ref, piece_ref):
    @pl.when(state_ref[0] == 1)
    def _():
        piece_ref[...] = shaped_piece(front_ref, high_ref, low_ref)


def round_piece(state, front, high, low, pieces):
    rank, wide = high.shape
    kept = front.shape[1]
    width = wide // pieces
    parts = 2 if width % 2048 == 0 else 1
    block = pl.BlockSpec(
        (rank, width // parts), lambda s, state: (0, (state[1] * parts + s) * state[0])
    )
    return pl.pallas_call(
        piece_body,
        grid_spec=pltpu.PrefetchScalarGridSpec(
            num_scalar_prefetch=1,
            grid=(parts,),
            in_specs=[fixed(rank, kept), block, block],
            out_specs=pl.BlockSpec((kept, width // parts), lambda s, state: (0, s * state[0])),
        ),
        out_shape=shape((kept, width)),
        name="round_piece",
        compiler_params=room(12),
    )(state, front, high, low)


def layout_body(pieces, scale, state_ref, *refs):
    sides, (out_ref, slots_ref, laid_ref, taken, placed) = (
        (refs[:pieces], refs[pieces : 2 * pieces]),
        refs[2 * pieces :],
    )
    vec = state_ref[1]
    for side in (0, 1):

        @pl.when(state_ref[2] == side)
        def _(side=side):
            copies = [
                pltpu.make_async_copy(sides[side][d], slots_ref.at[d], taken.at[d])
                for d in range(pieces)
            ]
            for copy in copies:
                copy.start()
            for copy in copies:
                copy.wait()

    kept, modes = laid_ref.shape[1:3]
    copies = []
    for d in range(pieces):
        stacked = jnp.stack(
            [slots_ref[d, :, i * kept : (i + 1) * kept] for i in range(modes)], axis=0
        )
        laid_ref[d] = stacked.transpose(1, 0, 2) * scale
        copies.append(pltpu.make_async_copy(laid_ref.at[d], out_ref.at[:, vec ^ d], placed.at[d]))
        copies[-1].start()
    for copy in copies:
        copy.wait()


def lay_out(state, first, last, scale):
    pieces = len(first)
    kept, width = first[0].shape
    modes = width // kept
    anywhere = pl.BlockSpec(memory_space=pl.ANY)
    return pl.pallas_call(
        functools.partial(layout_body, pieces, scale),
        in_specs=[SMEM] + [anywhere] * (2 * pieces),
        out_specs=anywhere,
        out_shape=shape((kept, pieces, modes, kept)),
        scratch_shapes=[
            pltpu.VMEM((pieces, kept, width), F32),
            pltpu.VMEM((pieces, kept, modes, kept), F32),
            pltpu.SemaphoreType.DMA((pieces,)),
            pltpu.SemaphoreType.DMA((pieces,)),
        ],
        name="lay_out",
        compiler_params=room(16),
    )(state, *first, *last)


def pair_list(count):
    return [(p, q) for p in range(count) for q in range(p, count)]


def chunk_rows(state_ref, half, d, chunks, kept):
    size = kept // (2 * chunks)
    start = (half * chunks + (state_ref[3] ^ d)) * size
    return (pl.multiple_of(start, 8) if size % 8 == 0 else start), size


def halves_of(state_ref, own_ref, other_ref):
    return (own_ref, state_ref[2]), (other_ref, 1 - state_ref[2])


def place_chunks(state_ref, own_ref, other_ref, out_ref):
    chunks, rows, kept = own_ref.shape
    for d in range(chunks):
        for ref, half in halves_of(state_ref, own_ref, other_ref):
            start, size = chunk_rows(state_ref, half, d, chunks, kept)
            for i in range(rows // size):
                out_ref[pl.ds(i * kept + start, size), :] = ref[d, i * size : (i + 1) * size, :]


def margin_body(count, state_ref, *refs):
    piece_refs, frame_anys, refs = refs[:count], refs[count : 2 * count], refs[2 * count :]
    own_any, other_any, _, keep_ref, give_ref, stage_ref, env_ref, out_ref = refs[:8]
    frame_ref, env_own_ref, env_other_ref, env_in_ref, copied = refs[8:]
    step = pl.program_id(0)
    pairs = pair_list(count)
    index_of = {pair: i for i, pair in enumerate(pairs)}

    @pl.when(state_ref[0] == 1)
    def _():
        me = state_ref[1]
        kept = piece_refs[0].shape[0]

        @pl.when(step == 0)
        def _():
            out_ref[...] = jnp.zeros_like(out_ref)

            @pl.when(state_ref[4] == 0)
            def _():
                copies = [
                    pltpu.make_async_copy(frame_anys[d], frame_ref.at[me ^ d], copied.at[d])
                    for d in range(count)
                ]
                for copy in copies:
                    copy.start()
                for copy in copies:
                    copy.wait()
                for i, (p, q) in enumerate(pairs):
                    env_in_ref[i * kept : (i + 1) * kept] = exact(frame_ref[p], frame_ref[q], 0, 0)

            @pl.when(state_ref[4] == 1)
            def _():
                copies = [
                    pltpu.make_async_copy(own_any, env_own_ref, copied.at[0]),
                    pltpu.make_async_copy(other_any, env_other_ref, copied.at[1]),
                ]
                for copy in copies:
                    copy.start()
                for copy in copies:
                    copy.wait()
                place_chunks(state_ref, env_own_ref, env_other_ref, env_in_ref)

            for i, (p, q) in enumerate(pairs):
                env = env_in_ref[i * kept : (i + 1) * kept]
                env_high, env_low = split(env)
                env_ref[q, p * kept : (p + 1) * kept, :kept] = env_high
                env_ref[q, p * kept : (p + 1) * kept, kept:] = env_low

        for d in range(count):
            stage_ref[me ^ d] = piece_refs[d][...]
        modes = piece_refs[0].shape[1] // kept

        def tall(value):
            return jnp.concatenate(
                [value[:, i * kept : (i + 1) * kept] for i in range(modes)], axis=0
            )

        highs, lows, carried = [], [], {}
        for q in range(count):
            high, low = split(stage_ref[q])
            highs.append(tall(high))
            lows.append(tall(low))
            rows = (q + 1) * kept
            env = env_ref[q, :rows]
            moved = contract(env, jnp.concatenate([high, high], axis=0), 1, 0) + contract(
                env, jnp.concatenate([low, low], axis=0), 1, 0
            )
            for p in range(q + 1):
                carried[p, q] = split(tall(moved[p * kept : (p + 1) * kept]))
        for p in range(count):
            partners = range(p, count)
            main = contract(
                jnp.concatenate([highs[p], lows[p]], axis=1),
                jnp.concatenate([carried[p, q][0] for q in partners], axis=1),
                0,
                0,
            )
            cross = contract(
                highs[p], jnp.concatenate([carried[p, q][1] for q in partners], axis=1), 0, 0
            )
            total = main[:kept] + (main[kept:] + cross)
            for j, q in enumerate(partners):
                i = index_of[p, q]
                out_ref[i * kept : (i + 1) * kept] += total[:, j * kept : (j + 1) * kept]

        @pl.when(step == pl.num_programs(0) - 1)
        def _():
            chunks, rows = keep_ref.shape[:2]
            for d in range(chunks):
                for ref, half in halves_of(state_ref, keep_ref, give_ref):
                    start, size = chunk_rows(state_ref, half, d, chunks, kept)
                    for i in range(rows // size):
                        ref[d, i * size : (i + 1) * size, :] = out_ref[
                            pl.ds(i * kept + start, size), :
                        ]


def margin_terms(state, pieces, frames, env, token):
    count = len(pieces)
    kept, wide = pieces[0].shape
    chunk = min(4 * kept, wide)
    total = count * (count + 1) // 2 * kept
    piece_spec = pl.BlockSpec((kept, chunk), lambda s, state: (0, s * state[0]))
    part = env[0].shape
    scratch = [
        pltpu.VMEM((count, kept, chunk), F32),
        pltpu.VMEM((count, count * kept, 2 * kept), BF16),
        pltpu.VMEM((total, kept), F32),
        pltpu.VMEM((count, *frames[0].shape), F32),
        pltpu.VMEM(part, F32),
        pltpu.VMEM(part, F32),
        pltpu.VMEM((total, kept), F32),
        pltpu.SemaphoreType.DMA((count,)),
    ]
    return pl.pallas_call(
        functools.partial(margin_body, count),
        grid_spec=pltpu.PrefetchScalarGridSpec(
            num_scalar_prefetch=1,
            grid=(wide // chunk,),
            in_specs=[piece_spec] * count + [ANY] * (count + 3),
            out_specs=[fixed(*part)] * 2,
            scratch_shapes=scratch,
        ),
        out_shape=[shape(part)] * 2,
        name="margin_terms",
        compiler_params=room(20),
    )(state, *pieces, *frames, *env, token)


def unset(dims):
    return pl.pallas_call(
        lambda ref: None, out_specs=ANY, out_shape=shape(dims), name="unset", compiler_params=room(2)
    )()


def pair_index(count, first, second):
    low, high = jnp.minimum(first, second), jnp.maximum(first, second)
    return low * count - low * (low - 1) // 2 + high - low


def owner_body(count, state_ref, *refs):
    part_refs, (out_ref, sum_ref) = refs[:-2], refs[-2:]
    sum_ref[...] = tree_sum([ref[...] for ref in part_refs])
    size = sum_ref.shape[0] // (count * (count + 1) // 2)
    for d in range(count):
        for q in range(count):
            start = pair_index(count, state_ref[1] ^ d, q) * size
            if size % 8 == 0:
                start = pl.multiple_of(start, 8)
            out_ref[d, q * size : (q + 1) * size, :] = sum_ref[pl.ds(start, size), :]


def owner_rows(state, parts, count):
    rows, kept = parts[0].shape
    size = rows // (count * (count + 1) // 2)
    return pl.pallas_call(
        functools.partial(owner_body, count),
        in_specs=[SMEM] + [VMEM] * len(parts),
        out_shape=shape((count, count * size, kept)),
        scratch_shapes=[pltpu.VMEM((rows, kept), F32)],
        name="owner_rows",
        compiler_params=room(4),
    )(state, *parts)


def pick_body(count, state_ref, own_ref, other_ref, own_row_ref, other_row_ref, out_ref, env_ref):
    kept = out_ref.shape[0]
    me = state_ref[1]

    @pl.when(state_ref[2] == 0)
    def _():
        place_chunks(state_ref, own_ref, other_ref, env_ref)
        for q in range(count):
            start = pl.multiple_of(pair_index(count, me, q) * kept, kept)
            block = env_ref[pl.ds(start, kept), :]
            out_ref[:, q * kept : (q + 1) * kept] = jnp.where(me > q, block.T, block)

    @pl.when(state_ref[2] == 1)
    def _():
        place_chunks(state_ref, own_row_ref, other_row_ref, env_ref)
        for q in range(count):
            block = env_ref[q * kept : (q + 1) * kept, :]
            out_ref[:, q * kept : (q + 1) * kept] = jnp.where(me > q, block.T, block)


def pick(state, env_first, env_last, count):
    kept = env_first[0].shape[2]
    return pl.pallas_call(
        functools.partial(pick_body, count),
        in_specs=[SMEM] + [VMEM] * 4,
        out_shape=shape((kept, count * kept)),
        scratch_shapes=[pltpu.VMEM((count * (count + 1) // 2 * kept, kept), F32)],
        name="pick",
        compiler_params=room(6),
    )(state, *env_first, *env_last)


def send(block, axis, size, distance):
    return lax.ppermute(block, axis, [(i, i ^ distance) for i in range(size)])


def swap(block):
    return send(block, "cores", 2, 1)


def send_from(block, side, size, distance):
    pairs = [(side * size + i, side * size + (i ^ distance)) for i in range(size)]
    return lax.ppermute(block, ("cores", "vec"), pairs)


def exchange_sum(block, axis, size):
    return tree_sum([block] + [send(block, axis, size, d) for d in range(1, size)])


def local(train_cores, sketch, exit_sketch):
    core = pltpu.with_memory_space_constraint(train_cores[0], pltpu.HBM)
    rank, mode_count, _ = core.shape
    kept = sketch.shape[1]
    row_size = lax.axis_size("row")
    vec_size = lax.axis_size("vec")
    side = lax.axis_index("cores")
    row = lax.axis_index("row")
    vec = lax.axis_index("vec")
    first_side = (side == 0).astype(jnp.int32)
    place = [vec, side, row]
    state_first = jnp.stack([first_side, *place, jnp.int32(0)])
    state_last = jnp.stack([1 - first_side, *place, jnp.int32(0)])
    state_next = jnp.stack([1 - first_side, *place, jnp.int32(1)])
    state_both = jnp.stack([jnp.int32(1), *place, jnp.int32(1)])
    scale = math.sqrt(kept * MODE)

    def row_total(keep, give, holder):
        mine = jnp.where(side == holder, keep, swap(give))
        own = exchange_sum(mine, "row", row_size)
        return own, swap(own)

    def row_parts(keep, give, holder):
        mine = jnp.where(side == holder, keep, swap(give))
        return [mine[0]] + [send(mine[d], "row", row_size, d) for d in range(1, row_size)]

    def row_collect(chunk):
        own = jnp.stack([chunk] + [send(chunk, "row", row_size, d) for d in range(1, row_size)])
        return own, swap(own)

    def env_total(keep, give, holder):
        return row_collect(exchange_sum(tree_sum(row_parts(keep, give, holder)), "vec", vec_size))

    def env_rows(keep, give, holder):
        rows = owner_rows(state_both, row_parts(keep, give, holder), vec_size)
        parts = [rows[0]] + [send(rows[d], "vec", vec_size, d) for d in range(1, vec_size)]
        return row_collect(tree_sum(parts))

    def at(state, d):
        return state.at[1].set(vec ^ d)

    def sent(pieces, holder, distances):
        for d in distances:
            pieces[d] = send_from(pieces[d], holder, vec_size, d)

    late = [vec_size // 2]
    pair_count = vec_size * (vec_size + 1) // 2
    blank = unset((row_size, pair_count * kept // (2 * row_size), kept))
    gram_first = row_total(*gram(state_first, core), 0)
    *gram_last, lower_own, inverse_own = absorbed_gram(state_last, gram_first, core)
    gram_last = row_total(*gram_last, 1)
    lower = jnp.where(side == 0, lower_own, swap(lower_own))
    inverse = jnp.where(side == 0, inverse_own, swap(inverse_own))
    exit_frame, _, _ = basis(state_last, gram_last, exit_sketch, lower_own, inverse_own)
    last_high, last_low, *left_last = project(state_last, core, exit_frame)
    left_last = row_total(*left_last, 1)
    other_sketch = swap(sketch)
    frame_last, front, map_first = basis(
        state_both, left_last, jnp.where(side == 1, sketch, other_sketch), lower, inverse
    )
    rounded_last = [front, last_high, last_low]
    if mode_count // vec_size % 8 == 0:
        first_high, first_low, *rest = project(
            state_first, core, map_first, rounded_last, vec_size
        )
        left_first, own_last = rest[:2], rest[2:]
    else:
        first_high, first_low, *left_first = project(state_first, core, map_first)
        own_last = [
            round_piece(at(state_last, d), *rounded_last, vec_size) for d in range(vec_size)
        ]
    first_high, first_low = (
        pltpu.with_memory_space_constraint(x, pltpu.HBM) for x in (first_high, first_low)
    )
    pieces_last = list(own_last)
    sent(pieces_last, 1, [d for d in range(1, vec_size) if d not in late])
    left_first = row_total(*left_first, 0)
    frame_first, _, _ = basis(state_first, left_first, sketch, lower, inverse)
    own_first = [None] * vec_size
    for d in range(vec_size - 1, -1, -1):
        own_first[d] = round_piece(at(state_first, d), frame_first, first_high, first_low, vec_size)
    pieces_first = list(own_first)
    sent(pieces_first, 0, range(1, vec_size))
    rounded = lay_out(state_both, own_first, own_last, scale)
    frames = [frame_first] + [send_from(frame_first, 0, vec_size, d) for d in range(1, vec_size)]
    held = [pieces_last[d] for d in late]
    token = swap(pieces_first[late[0]][:8, :128])
    for d, piece in zip(late, held):
        pieces_last[d] = piece
    sent(pieces_last, 1, late)
    env_first = margin_terms(state_first, pieces_first, frames, (blank, blank), token)
    env_first = env_total(*env_first, 0)
    env_last = env_rows(*margin_terms(state_next, pieces_last, frames, env_first, token), 1)
    margins = pick(state_both, env_first, env_last, vec_size)
    bases = jnp.where(side == 0, frame_first, frame_last) * math.sqrt(rank)
    return rounded.reshape(1, kept, mode_count, kept), bases[None], margins[None]


def solution(mesh):
    return jax.shard_map(
        local,
        mesh=mesh,
        in_specs=(P("vec", "cores", "row", None), P("cores", None), P()),
        out_specs=(
            P("vec", "cores", "row", None),
            P("vec", "cores", None),
            P("vec", "cores", None),
        ),
        check_vma=False,
    )
```
